256 devices in a mesh: depth: 256 (over y, z, x, core).
Axes of the slice: x: 4, y: 4, z: 8, core: 2. Of those that a mesh axis runs over, the one named last changes fastest.
Arguments:
- state_guess: float32 [256, 128, 512], P('depth'), may hold values from -6 to 6
- adjoint_guess: float32 [256, 128, 512], P('depth'), may hold values from -6 to 6
- w_in: bfloat16 [512, 512, 2048], P('depth'), may hold values from -0.25 to 0.25
- w_out: bfloat16 [512, 2048, 512], P('depth'), may hold values from -0.03125 to 0.03125
- norm_gain: float32 [512, 512], P('depth'), may hold values from 0.5 to 1.5
- decay: float32 [512, 512], P('depth'), may hold values from 0.5 to 1
Outputs:
- forward_states: float32 [512, 128, 512], P('depth')
- adjoint_states: float32 [512, 128, 512], P('depth')
The draws below stay inside these ranges and needn't reach their ends.
All inputs are finite; a program needn't handle non-finite values.
Results may differ from the reference program's by a relative error of at most 0.009.
Values sent between devices are 32-bit elements; how exact they have to be, the bound alone decides.
A program may use at most 192 MiB of HBM per device.

```python
import math
import jax
import jax.numpy as jnp
from jax import lax

D = 512
FF = 2048
TOK = 128
LOCAL = 2
COARSE = 256
BLOCKS = 512


def draw_decay(key, part):
    key_kind, key_spread, key_hit, key_drop = jax.random.split(key, 4)
    share = 0.5
    choose = jax.random.uniform(key_kind, (D,), jnp.float32)
    slow = choose < share
    spread = jnp.exp(jax.random.uniform(key_spread, (BLOCKS, D), jnp.float32, math.log(0.6), math.log(1.5)))
    rate = jnp.where(slow[None, :], math.log(2.0) / BLOCKS, 1.0 / 35.0) * spread
    hit = jax.random.uniform(key_hit, (BLOCKS, 1), jnp.float32) < 3.0 / BLOCKS
    drop = jax.random.uniform(key_drop, (BLOCKS, 1), jnp.float32, 0.6, 0.8)
    factor = jnp.where(hit, drop, 1.0)
    return (jnp.exp(-rate) * factor).astype(jnp.float32)


def level_of(stream_key, shape, cuts, smallest, high):
    loudness, own = 1.0, jax.random.fold_in(stream_key, 6)
    for dim, shards_of in cuts:
        draws = jnp.exp(jax.random.uniform(jax.random.fold_in(own, dim), (shards_of,), jnp.float32, smallest / len(cuts), high / len(cuts)))
        loudness = loudness * jnp.repeat(draws, shape[dim] // shards_of).reshape([-1 if axis == dim else 1 for axis in range(len(shape))])
    return loudness


def normal_values(own_key, extent, deviation, most, cuts=(), held_as=jnp.bfloat16):
    gain = level_of(own_key, extent, cuts, -0.22, 0.18) if cuts else 1.0
    values = jax.random.normal(own_key, extent, jnp.float32) * deviation * gain
    return jnp.minimum(jnp.maximum(values, -most), most).astype(held_as)


def setup_inputs(seed: int = 0) -> dict:
    seeds = jax.random.split(jax.random.key(seed), 7)
    state_guess = normal_values(seeds[0], (COARSE, TOK, D), 1.0, 6.0, ((0, 256),), jnp.float32)
    adjoint_guess = normal_values(seeds[1], (COARSE, TOK, D), 1.0, 6.0, ((0, 256),), jnp.float32)
    w_in = normal_values(seeds[2], (BLOCKS, D, FF), D ** -0.5, 0.25, ((0, 256),))
    w_out = normal_values(seeds[3], (BLOCKS, FF, D), (FF * 16) ** -0.5, 0.03125, ((0, 256),))
    norm_gain = jnp.clip(1.0 + 0.1 * jax.random.normal(seeds[4], (BLOCKS, D), jnp.float32), 0.5, 1.5)
    decay = draw_decay(jax.random.fold_in(seeds[6], 71), 0)
    return dict(state_guess=state_guess, adjoint_guess=adjoint_guess, w_in=w_in, w_out=w_out, norm_gain=norm_gain, decay=decay)


def prepare_block(state, w_first, gain_row):
    inverse = lax.rsqrt(lax.optimization_barrier(jnp.mean(state * state, axis=-1, keepdims=True)) + 1e-05)
    normed = (state * inverse * gain_row).astype(jnp.bfloat16)
    preact = jnp.dot(normed, w_first, preferred_element_type=jnp.float32)
    return (inverse, preact)

def finish_block(state, preact, w_second, decay_row):
    hidden = jax.nn.silu(preact).astype(jnp.bfloat16)
    return decay_row * state + jnp.dot(hidden, w_second, preferred_element_type=jnp.float32)

def backward_block(state, inverse, preact, upstream, w_first, w_second, gain_row, decay_row):
    grad_hidden = lax.dot_general(upstream.astype(jnp.bfloat16), w_second, (((1,), (1,)), ((), ())), preferred_element_type=jnp.float32)
    sigma = jax.nn.sigmoid(preact)
    grad_pre = (grad_hidden * sigma * (1.0 + preact * (1.0 - sigma))).astype(jnp.bfloat16)
    grad_norm = lax.dot_general(grad_pre, w_first, (((1,), (1,)), ((), ())), preferred_element_type=jnp.float32)
    scaled = grad_norm * gain_row
    inner = lax.optimization_barrier(jnp.mean(scaled * state, axis=-1, keepdims=True))
    return decay_row * upstream + inverse * scaled - state * inverse ** 3 * inner

def relax_forward(start, w_first, w_second, gains, decays, want_end):
    state = start
    count = w_first.shape[0]
    states_list, inverse_list, preact_list = ([], [], [])
    for block in range(count):
        states_list.append(state)
        inverse, preact = prepare_block(state, w_first[block], gains[block])
        inverse_list.append(inverse)
        preact_list.append(preact)
        if want_end or block + 1 < count:
            state = finish_block(state, preact, w_second[block], decays[block])
    return (state, jnp.stack(states_list), jnp.stack(inverse_list), jnp.stack(preact_list))

def relax_backward(start, states, inverses, preacts, w_first, w_second, gains, decays):
    adjoint = start
    count = w_first.shape[0]
    collected = [None] * count
    for block in reversed(range(count)):
        adjoint = backward_block(states[block], inverses[block], preacts[block], adjoint, w_first[block], w_second[block], gains[block], decays[block])
        collected[block] = adjoint
    return (adjoint, jnp.stack(collected))

def reference(state_guess, adjoint_guess, w_in, w_out, norm_gain, decay):
    first_r = w_in.reshape(COARSE, LOCAL, D, FF)
    second_r = w_out.reshape(COARSE, LOCAL, FF, D)
    gain_r = norm_gain.reshape(COARSE, LOCAL, D)
    decay_r = decay.reshape(COARSE, LOCAL, D)
    factors = jnp.prod(decay_r, axis=1)
    zero_row = jnp.zeros((1, TOK, D), jnp.float32)
    ends = lax.map(lambda items: relax_forward(*items, True)[0], (state_guess, first_r, second_r, gain_r, decay_r))
    resid = jnp.concatenate([zero_row, ends[:-1] - state_guess[1:]], axis=0)

    def forward_step(carry, items):
        factor_prev, resid_now = items
        carry = factor_prev * carry + resid_now
        return (carry, carry)
    _, corr = lax.scan(forward_step, jnp.zeros((TOK, D), jnp.float32), (factors[:-1], resid[1:]))
    starts = state_guess + jnp.concatenate([zero_row, corr], axis=0)
    states, inverses, preacts = lax.map(lambda items: relax_forward(*items, False)[1:], (starts, first_r, second_r, gain_r, decay_r))
    firsts = lax.map(lambda items: relax_backward(*items)[0], (adjoint_guess, states, inverses, preacts, first_r, second_r, gain_r, decay_r))
    rho = jnp.concatenate([firsts[1:] - adjoint_guess[:-1], zero_row], axis=0)

    def backward_step(carry, items):
        factor_next, rho_now = items
        carry = factor_next * carry + rho_now
        return (carry, carry)
    _, eps = lax.scan(backward_step, jnp.zeros((TOK, D), jnp.float32), (factors[1:], rho[:-1]), reverse=True)
    heads = adjoint_guess + jnp.concatenate([eps, zero_row], axis=0)
    lambdas = lax.map(lambda items: relax_backward(*items)[1], (heads, states, inverses, preacts, first_r, second_r, gain_r, decay_r))
    return (states.reshape(BLOCKS, TOK, D), lambdas.reshape(BLOCKS, TOK, D))
```

```python
import jax
import jax.numpy as jnp
from jax import lax
from jax.sharding import PartitionSpec as P


def shifted(block, axis, distance):
    devices = range(lax.axis_size(axis))
    route = [(i - distance, i) for i in devices if i - distance in devices]
    return lax.ppermute(block, axis, route)


def doubling_scan(factor, offset, axis, reverse):
    size, position = (lax.axis_size(axis), lax.axis_index(axis))
    rows = offset.shape[0]
    packed = jnp.concatenate([offset, factor[None, :]], axis=0)
    distance = 1
    while distance < size:
        step = -distance if reverse else distance
        came = shifted(packed, axis, step)
        reached = position + distance < size if reverse else position >= distance
        scale = packed[rows:]
        joined = jnp.concatenate(
            [packed[:rows] + scale * came[:rows], scale * came[rows:]], axis=0
        )
        packed = jnp.where(reached, joined, packed)
        distance *= 2
    return packed[:rows]


def prepare_block(state, w_first, gain_row):
    inverse = lax.rsqrt(jnp.mean(state * state, axis=-1, keepdims=True) + 1e-05)
    normed = (state * inverse * gain_row).astype(jnp.bfloat16)
    preact = jnp.dot(normed, w_first, preferred_element_type=jnp.float32)
    return (inverse, preact)


def finish_block(state, preact, w_second, decay_row):
    hidden = jax.nn.silu(preact).astype(jnp.bfloat16)
    return decay_row * state + jnp.dot(hidden, w_second, preferred_element_type=jnp.float32)


def backward_block(state, inverse, preact, upstream, w_first, w_second, gain_row, decay_row):
    grad_hidden = lax.dot_general(
        upstream.astype(jnp.bfloat16),
        w_second,
        (((1,), (1,)), ((), ())),
        preferred_element_type=jnp.float32,
    )
    sigma = jax.nn.sigmoid(preact)
    grad_pre = (grad_hidden * sigma * (1.0 + preact * (1.0 - sigma))).astype(jnp.bfloat16)
    grad_norm = lax.dot_general(
        grad_pre, w_first, (((1,), (1,)), ((), ())), preferred_element_type=jnp.float32
    )
    scaled = grad_norm * gain_row
    inner = jnp.mean(scaled * state, axis=-1, keepdims=True)
    return decay_row * upstream + inverse * scaled - state * inverse**3 * inner


def relax_forward(start, w_in, w_out, norm_gain, decay, want_end):
    state = start
    count = w_in.shape[0]
    states_list, inverse_list, preact_list = ([], [], [])
    for block in range(count):
        states_list.append(state)
        inverse, preact = prepare_block(state, w_in[block], norm_gain[block])
        inverse_list.append(inverse)
        preact_list.append(preact)
        if want_end or block + 1 < count:
            state = finish_block(state, preact, w_out[block], decay[block])
    return (state, states_list, inverse_list, preact_list)


def relax_backward(start, states, inverses, preacts, w_in, w_out, norm_gain, decay):
    adjoint = start
    count = w_in.shape[0]
    collected = [None] * count
    for block in reversed(range(count)):
        adjoint = backward_block(
            states[block],
            inverses[block],
            preacts[block],
            adjoint,
            w_in[block],
            w_out[block],
            norm_gain[block],
            decay[block],
        )
        collected[block] = adjoint
    return (adjoint, collected)


def compose(earlier, later):
    return (later[0] * earlier[0], later[0] * earlier[1] + later[1])


def shards(state_guess, adjoint_guess, w_in, w_out, norm_gain, decay):
    position = lax.axis_index("depth")
    devices = lax.axis_size("depth")
    factor = jnp.prod(decay, axis=0)
    at_first = position == 0
    at_last = position == devices - 1
    factor_before = shifted(factor, "depth", 1)
    factor_after = shifted(factor, "depth", -1)
    guess_state = state_guess[0]
    end_state, _, _, _ = relax_forward(guess_state, w_in, w_out, norm_gain, decay, True)
    end_before = shifted(end_state, "depth", 1)
    resid = jnp.where(at_first, jnp.zeros_like(guess_state), end_before - guess_state)
    correction = doubling_scan(factor_before, resid, "depth", False)
    start = guess_state + correction
    _, states, inverses, preacts = relax_forward(start, w_in, w_out, norm_gain, decay, False)
    guess_adjoint = adjoint_guess[0]
    first_adjoint, _ = relax_backward(
        guess_adjoint, states, inverses, preacts, w_in, w_out, norm_gain, decay
    )
    first_after = shifted(first_adjoint, "depth", -1)
    rho = jnp.where(at_last, jnp.zeros_like(guess_adjoint), first_after - guess_adjoint)
    eps = doubling_scan(factor_after, rho, "depth", True)
    head = guess_adjoint + eps
    _, lambdas = relax_backward(head, states, inverses, preacts, w_in, w_out, norm_gain, decay)
    return (jnp.stack(states), jnp.stack(lambdas))


def solution(mesh):
    placed = (
        P("depth", None, None),
        P("depth", None, None),
        P("depth", None, None),
        P("depth", None, None),
        P("depth", None),
        P("depth", None),
    )
    return jax.shard_map(
        shards,
        mesh=mesh,
        in_specs=placed,
        out_specs=(P("depth", None, None), P("depth", None, None)),
        check_vma=False,
    )
```

```python
import jax
import jax.numpy as jnp
from jax import lax
from jax.sharding import PartitionSpec as P


def shifted(block, axis, distance):
    devices = range(lax.axis_size(axis))
    route = [(i - distance, i) for i in devices if i - distance in devices]
    return lax.ppermute(block, axis, route)


def later_of(later, earlier, rows):
    scale = later[rows:]
    return jnp.concatenate([later[:rows] + scale * earlier[:rows], scale * earlier[rows:]], axis=0)


def chip_scan(factor, offset, axis, reverse):
    size, position = (lax.axis_size(axis), lax.axis_index(axis))
    rows, width = offset.shape
    half = width // 2
    order = size - 1 - position if reverse else position
    core, chip = (order % 2, order // 2)

    def placed(q):
        return size - 1 - q if reverse else q

    def move(block, pairs):
        return lax.ppermute(block, axis, [(placed(a), placed(b)) for a, b in pairs])

    packed = jnp.concatenate([offset, factor[None, :]], axis=0)
    mine = lax.dynamic_slice_in_dim(packed, core * half, half, axis=1)
    other = lax.dynamic_slice_in_dim(packed, (1 - core) * half, half, axis=1)
    swap = [(q, q + 1) for q in range(0, size, 2)] + [(q + 1, q) for q in range(0, size, 2)]
    got = move(other, swap)
    first = core == 0
    total = later_of(jnp.where(first, got, mine), jnp.where(first, mine, got), rows)
    chips = size // 2
    distance = 1
    while distance < chips:
        came = move(total, [(q, q + 2 * distance) for q in range(size - 2 * distance)])
        total = jnp.where(chip >= distance, later_of(total, came, rows), total)
        distance *= 2
    near = move(total, [(q, q + 1) for q in range(size - 1)])
    far = move(total, [(q, q + 2) for q in range(0, size - 2, 2)])
    second_full = jnp.concatenate([near[:rows], total[:rows]], axis=1)
    before = jnp.concatenate([far[:rows], near[:rows]], axis=1)
    first_full = jnp.where(chip >= 1, offset + factor[None, :] * before, offset)
    return jnp.where(first, first_full, second_full)


def prepare_block(state, w_first, gain_row):
    inverse = lax.rsqrt(jnp.mean(state * state, axis=-1, keepdims=True) + 1e-05)
    normed = (state * inverse * gain_row).astype(jnp.bfloat16)
    preact = jnp.dot(normed, w_first, preferred_element_type=jnp.float32)
    return (inverse, preact)


def finish_block(state, preact, w_second, decay_row):
    hidden = jax.nn.silu(preact).astype(jnp.bfloat16)
    return decay_row * state + jnp.dot(hidden, w_second, preferred_element_type=jnp.float32)


def backward_block(state, inverse, preact, upstream, w_first, w_second, gain_row, decay_row):
    grad_hidden = lax.dot_general(
        upstream.astype(jnp.bfloat16),
        w_second,
        (((1,), (1,)), ((), ())),
        preferred_element_type=jnp.float32,
    )
    sigma = jax.nn.sigmoid(preact)
    grad_pre = (grad_hidden * sigma * (1.0 + preact * (1.0 - sigma))).astype(jnp.bfloat16)
    grad_norm = lax.dot_general(
        grad_pre, w_first, (((1,), (1,)), ((), ())), preferred_element_type=jnp.float32
    )
    scaled = grad_norm * gain_row
    inner = jnp.mean(scaled * state, axis=-1, keepdims=True)
    return decay_row * upstream + inverse * scaled - state * inverse**3 * inner


def relax_forward(start, w_in, w_out, norm_gain, decay, want_end):
    state = start
    count = w_in.shape[0]
    states_list, inverse_list, preact_list = ([], [], [])
    for block in range(count):
        states_list.append(state)
        inverse, preact = prepare_block(state, w_in[block], norm_gain[block])
        inverse_list.append(inverse)
        preact_list.append(preact)
        if want_end or block + 1 < count:
            state = finish_block(state, preact, w_out[block], decay[block])
    return (state, states_list, inverse_list, preact_list)


def relax_backward(start, states, inverses, preacts, w_in, w_out, norm_gain, decay):
    adjoint = start
    count = w_in.shape[0]
    collected = [None] * count
    for block in reversed(range(count)):
        adjoint = backward_block(
            states[block],
            inverses[block],
            preacts[block],
            adjoint,
            w_in[block],
            w_out[block],
            norm_gain[block],
            decay[block],
        )
        collected[block] = adjoint
    return (adjoint, collected)


def compose(earlier, later):
    return (later[0] * earlier[0], later[0] * earlier[1] + later[1])


def shards(state_guess, adjoint_guess, w_in, w_out, norm_gain, decay):
    position = lax.axis_index("depth")
    devices = lax.axis_size("depth")
    factor = jnp.prod(decay, axis=0)
    at_first = position == 0
    at_last = position == devices - 1
    factor_before = shifted(factor, "depth", 1)
    factor_after = shifted(factor, "depth", -1)
    guess_state = state_guess[0]
    end_state, _, _, _ = relax_forward(guess_state, w_in, w_out, norm_gain, decay, True)
    end_before = shifted(end_state, "depth", 1)
    resid = jnp.where(at_first, jnp.zeros_like(guess_state), end_before - guess_state)
    correction = chip_scan(factor_before, resid, "depth", False)
    start = guess_state + correction
    _, states, inverses, preacts = relax_forward(start, w_in, w_out, norm_gain, decay, False)
    guess_adjoint = adjoint_guess[0]
    first_adjoint, _ = relax_backward(
        guess_adjoint, states, inverses, preacts, w_in, w_out, norm_gain, decay
    )
    first_after = shifted(first_adjoint, "depth", -1)
    rho = jnp.where(at_last, jnp.zeros_like(guess_adjoint), first_after - guess_adjoint)
    eps = chip_scan(factor_after, rho, "depth", True)
    head = guess_adjoint + eps
    _, lambdas = relax_backward(head, states, inverses, preacts, w_in, w_out, norm_gain, decay)
    return (jnp.stack(states), jnp.stack(lambdas))


def solution(mesh):
    placed = (
        P("depth", None, None),
        P("depth", None, None),
        P("depth", None, None),
        P("depth", None, None),
        P("depth", None),
        P("depth", None),
    )
    return jax.shard_map(
        shards,
        mesh=mesh,
        in_specs=placed,
        out_specs=(P("depth", None, None), P("depth", None, None)),
        check_vma=False,
    )
```

```python
import functools

import jax
import jax.numpy as jnp
from jax import lax
from jax.experimental import pallas as pl
from jax.experimental.pallas import tpu as pltpu
from jax.sharding import PartitionSpec as P


def shifted(block, axis, distance):
    devices = range(lax.axis_size(axis))
    route = [(i - distance, i) for i in devices if i - distance in devices]
    return lax.ppermute(block, axis, route)


MESH = pl.DeviceIdType.MESH


def joined(later, earlier, rows):
    scale = later[rows : rows + 1, :]
    top = later[:rows, :] + scale * earlier[:rows, :]
    return jnp.concatenate([top, later[rows:, :] * earlier[rows:, :]], axis=0)


def scan_kernel(size, reverse, mine_ref, other_ref, offset_ref, factor_ref, out_ref, got, total, sends, recvs):
    position = lax.axis_index("depth")
    order = size - 1 - position if reverse else position
    core, chip = (order % 2, order // 2)
    rows = offset_ref.shape[0]
    half = mine_ref.shape[1]
    chips = size // 2
    hops = []
    distance = 1
    while distance < chips:
        hops.append(2 * distance)
        distance *= 2

    def device(q):
        q = lax.rem(q + 2 * size, size)
        return (size - 1 - q if reverse else q,)

    partner = order + 1 - 2 * core
    barrier = pltpu.get_barrier_semaphore()
    targets = [partner] + [order + h for h in hops] + [order - h for h in hops]
    targets += [order + 1, order - 1, order + 2, order - 2]
    for target in targets:
        pl.semaphore_signal(barrier, inc=1, device_id=device(target), device_id_type=MESH)
    pl.semaphore_wait(barrier, len(targets))

    def send(src, slot, target):
        copy = pltpu.make_async_remote_copy(
            src_ref=src,
            dst_ref=got.at[slot],
            send_sem=sends.at[slot],
            recv_sem=recvs.at[slot],
            device_id=device(target),
            device_id_type=MESH,
        )
        copy.start()
        return copy

    send(other_ref, 0, partner).wait()
    first = core == 0
    mine = mine_ref[...]
    came = got[0]
    total[0] = joined(jnp.where(first, came, mine), jnp.where(first, mine, came), rows)
    for step, hop in enumerate(hops):
        send(total.at[step], step + 1, order + hop).wait()
        held = total[step]
        total[step + 1] = jnp.where(chip >= hop // 2, joined(held, got[step + 1], rows), held)
    last = len(hops)
    near = send(total.at[last], last + 1, order + 1)
    far = send(total.at[last], last + 2, order + 2)
    near.wait()
    far.wait()
    close = got[last + 1, :rows, :]
    own = total[last, :rows, :]
    before_left = got[last + 2, :rows, :]
    offset_left = offset_ref[:, :half]
    offset_right = offset_ref[:, half:]
    factor_left = factor_ref[0:1, :half]
    factor_right = factor_ref[0:1, half:]
    early = chip >= 1
    out_ref[:, :half] = jnp.where(
        first, jnp.where(early, offset_left + factor_left * before_left, offset_left), close
    )
    out_ref[:, half:] = jnp.where(
        first, jnp.where(early, offset_right + factor_right * close, offset_right), own
    )


def kernel_scan(factor, offset, reverse, ident):
    size, position = (lax.axis_size("depth"), lax.axis_index("depth"))
    rows, width = offset.shape
    half = width // 2
    order = size - 1 - position if reverse else position
    core = order % 2
    spread = jnp.broadcast_to(factor[None, :], (8, width))
    packed = jnp.concatenate([offset, spread], axis=0)
    mine = lax.dynamic_slice_in_dim(packed, core * half, half, axis=1)
    other = lax.dynamic_slice_in_dim(packed, (1 - core) * half, half, axis=1)
    stages = 3 + (size // 2).bit_length() - 1
    return pl.pallas_call(
        functools.partial(scan_kernel, size, reverse),
        out_shape=jax.ShapeDtypeStruct((rows, width), jnp.float32),
        in_specs=[pl.BlockSpec(memory_space=pltpu.VMEM)] * 4,
        out_specs=pl.BlockSpec(memory_space=pltpu.VMEM),
        scratch_shapes=[
            pltpu.VMEM((stages, rows + 8, half), jnp.float32),
            pltpu.VMEM((stages - 2, rows + 8, half), jnp.float32),
            pltpu.SemaphoreType.DMA((stages,)),
            pltpu.SemaphoreType.DMA((stages,)),
        ],
        compiler_params=pltpu.CompilerParams(collective_id=ident, has_side_effects=True),
    )(mine, other, offset, spread)


def prepare_block(state, w_first, gain_row):
    inverse = lax.rsqrt(jnp.mean(state * state, axis=-1, keepdims=True) + 1e-05)
    normed = (state * inverse * gain_row).astype(jnp.bfloat16)
    preact = jnp.dot(normed, w_first, preferred_element_type=jnp.float32)
    return (inverse, preact)


def finish_block(state, preact, w_second, decay_row):
    hidden = jax.nn.silu(preact).astype(jnp.bfloat16)
    return decay_row * state + jnp.dot(hidden, w_second, preferred_element_type=jnp.float32)


def backward_block(state, inverse, preact, upstream, w_first, w_second, gain_row, decay_row):
    grad_hidden = lax.dot_general(
        upstream.astype(jnp.bfloat16),
        w_second,
        (((1,), (1,)), ((), ())),
        preferred_element_type=jnp.float32,
    )
    sigma = jax.nn.sigmoid(preact)
    grad_pre = (grad_hidden * sigma * (1.0 + preact * (1.0 - sigma))).astype(jnp.bfloat16)
    grad_norm = lax.dot_general(
        grad_pre, w_first, (((1,), (1,)), ((), ())), preferred_element_type=jnp.float32
    )
    scaled = grad_norm * gain_row
    inner = jnp.mean(scaled * state, axis=-1, keepdims=True)
    return decay_row * upstream + inverse * scaled - state * inverse**3 * inner


def relax_forward(start, w_in, w_out, norm_gain, decay, want_end):
    state = start
    count = w_in.shape[0]
    states_list, inverse_list, preact_list = ([], [], [])
    for block in range(count):
        states_list.append(state)
        inverse, preact = prepare_block(state, w_in[block], norm_gain[block])
        inverse_list.append(inverse)
        preact_list.append(preact)
        if want_end or block + 1 < count:
            state = finish_block(state, preact, w_out[block], decay[block])
    return (state, states_list, inverse_list, preact_list)


def relax_backward(start, states, inverses, preacts, w_in, w_out, norm_gain, decay):
    adjoint = start
    count = w_in.shape[0]
    collected = [None] * count
    for block in reversed(range(count)):
        adjoint = backward_block(
            states[block],
            inverses[block],
            preacts[block],
            adjoint,
            w_in[block],
            w_out[block],
            norm_gain[block],
            decay[block],
        )
        collected[block] = adjoint
    return (adjoint, collected)


def compose(earlier, later):
    return (later[0] * earlier[0], later[0] * earlier[1] + later[1])


def shards(state_guess, adjoint_guess, w_in, w_out, norm_gain, decay):
    position = lax.axis_index("depth")
    devices = lax.axis_size("depth")
    factor = jnp.prod(decay, axis=0)
    at_first = position == 0
    at_last = position == devices - 1
    factor_before = shifted(factor, "depth", 1)
    factor_after = shifted(factor, "depth", -1)
    guess_state = state_guess[0]
    end_state, _, _, _ = relax_forward(guess_state, w_in, w_out, norm_gain, decay, True)
    end_before = shifted(end_state, "depth", 1)
    resid = jnp.where(at_first, jnp.zeros_like(guess_state), end_before - guess_state)
    correction = kernel_scan(factor_before, resid, False, 0)
    start = guess_state + correction
    _, states, inverses, preacts = relax_forward(start, w_in, w_out, norm_gain, decay, False)
    guess_adjoint = adjoint_guess[0]
    first_adjoint, _ = relax_backward(
        guess_adjoint, states, inverses, preacts, w_in, w_out, norm_gain, decay
    )
    first_after = shifted(first_adjoint, "depth", -1)
    rho = jnp.where(at_last, jnp.zeros_like(guess_adjoint), first_after - guess_adjoint)
    eps = kernel_scan(factor_after, rho, True, 1)
    head = guess_adjoint + eps
    _, lambdas = relax_backward(head, states, inverses, preacts, w_in, w_out, norm_gain, decay)
    return (jnp.stack(states), jnp.stack(lambdas))


def solution(mesh):
    placed = (
        P("depth", None, None),
        P("depth", None, None),
        P("depth", None, None),
        P("depth", None, None),
        P("depth", None),
        P("depth", None),
    )
    return jax.shard_map(
        shards,
        mesh=mesh,
        in_specs=placed,
        out_specs=(P("depth", None, None), P("depth", None, None)),
        check_vma=False,
    )
```

```python
import functools

import jax
import jax.numpy as jnp
from jax import lax
from jax.experimental import pallas as pl
from jax.experimental.pallas import tpu as pltpu
from jax.sharding import PartitionSpec as P


def shifted(block, axis, distance):
    devices = range(lax.axis_size(axis))
    route = [(i - distance, i) for i in devices if i - distance in devices]
    return lax.ppermute(block, axis, route)


MESH = pl.DeviceIdType.MESH


def scan_kernel(size, reverse, pieces, mine_ref, other_ref, offset_ref, factor_ref, out_ref, got, total, sends, recvs):
    position = lax.axis_index("depth")
    order = size - 1 - position if reverse else position
    core, chip = (order % 2, order // 2)
    rows = offset_ref.shape[0]
    half = mine_ref.shape[1]
    chips = size // 2
    step_rows = rows // pieces
    spans = [(rows, 8)] + [(k * step_rows, step_rows) for k in range(pieces)]
    hops = []
    distance = 1
    while distance < chips:
        hops.append(2 * distance)
        distance *= 2

    def device(q):
        q = lax.rem(q + 2 * size, size)
        return (size - 1 - q if reverse else q,)

    partner = order + 1 - 2 * core
    barrier = pltpu.get_barrier_semaphore()
    targets = [partner] + [order + h for h in hops] + [order - h for h in hops]
    targets += [order + 1, order - 1, order + 2, order - 2]
    for target in targets:
        pl.semaphore_signal(barrier, inc=1, device_id=device(target), device_id_type=MESH)
    pl.semaphore_wait(barrier, len(targets))

    started = []

    def send(src, slot, piece, target):
        first_row, count = spans[piece]
        copy = pltpu.make_async_remote_copy(
            src_ref=src.at[pl.ds(first_row, count), :],
            dst_ref=got.at[slot].at[pl.ds(first_row, count), :],
            send_sem=sends.at[slot, piece],
            recv_sem=recvs.at[slot, piece],
            device_id=device(target),
            device_id_type=MESH,
        )
        copy.start()
        started.append(copy)
        return copy

    first = core == 0
    pending = [send(other_ref, 0, piece, partner) for piece in range(pieces + 1)]
    factor_row = slice(rows, rows + 1)
    for stage in range(len(hops) + 1):
        following = []
        for piece in range(pieces + 1):
            first_row, count = spans[piece]
            part = slice(first_row, first_row + count)
            pending[piece].wait_recv()
            came = got[stage, part, :]
            if stage == 0:
                mine = mine_ref[part, :]
                later = jnp.where(first, came, mine)
                earlier = jnp.where(first, mine, came)
                scale = jnp.where(first, got[0, factor_row, :], mine_ref[factor_row, :])
                if piece == 0:
                    value = later * earlier
                else:
                    value = later + scale * earlier
            else:
                held = total[stage - 1, part, :]
                scale = total[stage - 1, factor_row, :]
                if piece == 0:
                    combined = held * came
                else:
                    combined = held + scale * came
                value = jnp.where(chip >= hops[stage - 1] // 2, combined, held)
            total[stage, part, :] = value
            if stage < len(hops):
                following.append(send(total.at[stage], stage + 1, piece, order + hops[stage]))
        pending = following
    last = len(hops)
    near = [None] + [send(total.at[last], last + 1, piece, order + 1) for piece in range(1, pieces + 1)]
    far = [None] + [send(total.at[last], last + 2, piece, order + 2) for piece in range(1, pieces + 1)]
    early = chip >= 1
    for piece in range(1, pieces + 1):
        first_row, count = spans[piece]
        part = slice(first_row, first_row + count)
        near[piece].wait_recv()
        far[piece].wait_recv()
        close = got[last + 1, part, :]
        own = total[last, part, :]
        before_left = got[last + 2, part, :]
        offset_left = offset_ref[part, :half]
        offset_right = offset_ref[part, half:]
        out_ref[part, :half] = jnp.where(
            first,
            jnp.where(early, offset_left + factor_ref[0:1, :half] * before_left, offset_left),
            close,
        )
        out_ref[part, half:] = jnp.where(
            first,
            jnp.where(early, offset_right + factor_ref[0:1, half:] * close, offset_right),
            own,
        )
    for copy in started:
        copy.wait_send()


def kernel_scan(factor, offset, reverse, ident):
    size, position = (lax.axis_size("depth"), lax.axis_index("depth"))
    rows, width = offset.shape
    half = width // 2
    order = size - 1 - position if reverse else position
    core = order % 2
    spread = jnp.broadcast_to(factor[None, :], (8, width))
    packed = jnp.concatenate([offset, spread], axis=0)
    mine = lax.dynamic_slice_in_dim(packed, core * half, half, axis=1)
    other = lax.dynamic_slice_in_dim(packed, (1 - core) * half, half, axis=1)
    stages = 3 + (size // 2).bit_length() - 1
    return pl.pallas_call(
        functools.partial(scan_kernel, size, reverse, 4),
        out_shape=jax.ShapeDtypeStruct((rows, width), jnp.float32),
        in_specs=[pl.BlockSpec(memory_space=pltpu.VMEM)] * 4,
        out_specs=pl.BlockSpec(memory_space=pltpu.VMEM),
        scratch_shapes=[
            pltpu.VMEM((stages, rows + 8, half), jnp.float32),
            pltpu.VMEM((stages - 2, rows + 8, half), jnp.float32),
            pltpu.SemaphoreType.DMA((stages, 5)),
            pltpu.SemaphoreType.DMA((stages, 5)),
        ],
        compiler_params=pltpu.CompilerParams(collective_id=ident, has_side_effects=True),
    )(mine, other, offset, spread)


def prepare_block(state, w_first, gain_row):
    inverse = lax.rsqrt(jnp.mean(state * state, axis=-1, keepdims=True) + 1e-05)
    normed = (state * inverse * gain_row).astype(jnp.bfloat16)
    preact = jnp.dot(normed, w_first, preferred_element_type=jnp.float32)
    return (inverse, preact)


def finish_block(state, preact, w_second, decay_row):
    hidden = jax.nn.silu(preact).astype(jnp.bfloat16)
    return decay_row * state + jnp.dot(hidden, w_second, preferred_element_type=jnp.float32)


def backward_block(state, inverse, preact, upstream, w_first, w_second, gain_row, decay_row):
    grad_hidden = lax.dot_general(
        upstream.astype(jnp.bfloat16),
        w_second,
        (((1,), (1,)), ((), ())),
        preferred_element_type=jnp.float32,
    )
    sigma = jax.nn.sigmoid(preact)
    grad_pre = (grad_hidden * sigma * (1.0 + preact * (1.0 - sigma))).astype(jnp.bfloat16)
    grad_norm = lax.dot_general(
        grad_pre, w_first, (((1,), (1,)), ((), ())), preferred_element_type=jnp.float32
    )
    scaled = grad_norm * gain_row
    inner = jnp.mean(scaled * state, axis=-1, keepdims=True)
    return decay_row * upstream + inverse * scaled - state * inverse**3 * inner


def relax_forward(start, w_in, w_out, norm_gain, decay, want_end):
    state = start
    count = w_in.shape[0]
    states_list, inverse_list, preact_list = ([], [], [])
    for block in range(count):
        states_list.append(state)
        inverse, preact = prepare_block(state, w_in[block], norm_gain[block])
        inverse_list.append(inverse)
        preact_list.append(preact)
        if want_end or block + 1 < count:
            state = finish_block(state, preact, w_out[block], decay[block])
    return (state, states_list, inverse_list, preact_list)


def relax_backward(start, states, inverses, preacts, w_in, w_out, norm_gain, decay):
    adjoint = start
    count = w_in.shape[0]
    collected = [None] * count
    for block in reversed(range(count)):
        adjoint = backward_block(
            states[block],
            inverses[block],
            preacts[block],
            adjoint,
            w_in[block],
            w_out[block],
            norm_gain[block],
            decay[block],
        )
        collected[block] = adjoint
    return (adjoint, collected)


def compose(earlier, later):
    return (later[0] * earlier[0], later[0] * earlier[1] + later[1])


def shards(state_guess, adjoint_guess, w_in, w_out, norm_gain, decay):
    position = lax.axis_index("depth")
    devices = lax.axis_size("depth")
    factor = jnp.prod(decay, axis=0)
    at_first = position == 0
    at_last = position == devices - 1
    factor_before = shifted(factor, "depth", 1)
    factor_after = shifted(factor, "depth", -1)
    guess_state = state_guess[0]
    end_state, _, _, _ = relax_forward(guess_state, w_in, w_out, norm_gain, decay, True)
    end_before = shifted(end_state, "depth", 1)
    resid = jnp.where(at_first, jnp.zeros_like(guess_state), end_before - guess_state)
    correction = kernel_scan(factor_before, resid, False, 0)
    start = guess_state + correction
    _, states, inverses, preacts = relax_forward(start, w_in, w_out, norm_gain, decay, False)
    guess_adjoint = adjoint_guess[0]
    first_adjoint, _ = relax_backward(
        guess_adjoint, states, inverses, preacts, w_in, w_out, norm_gain, decay
    )
    first_after = shifted(first_adjoint, "depth", -1)
    rho = jnp.where(at_last, jnp.zeros_like(guess_adjoint), first_after - guess_adjoint)
    eps = kernel_scan(factor_after, rho, True, 1)
    head = guess_adjoint + eps
    _, lambdas = relax_backward(head, states, inverses, preacts, w_in, w_out, norm_gain, decay)
    return (jnp.stack(states), jnp.stack(lambdas))


def solution(mesh):
    placed = (
        P("depth", None, None),
        P("depth", None, None),
        P("depth", None, None),
        P("depth", None, None),
        P("depth", None),
        P("depth", None),
    )
    return jax.shard_map(
        shards,
        mesh=mesh,
        in_specs=placed,
        out_specs=(P("depth", None, None), P("depth", None, None)),
        check_vma=False,
    )
```

```python
import functools

import jax
import jax.numpy as jnp
from jax import lax
from jax.experimental import pallas as pl
from jax.experimental.pallas import tpu as pltpu
from jax.sharding import PartitionSpec as P


def shifted(block, axis, distance):
    devices = range(lax.axis_size(axis))
    route = [(i - distance, i) for i in devices if i - distance in devices]
    return lax.ppermute(block, axis, route)


MESH = pl.DeviceIdType.MESH


def scan_kernel(size, reverse, pieces, mine_ref, other_ref, offset_ref, factor_ref, out_ref, got, total, sends, recvs):
    position = lax.axis_index("depth")
    order = size - 1 - position if reverse else position
    core, chip = (order % 2, order // 2)
    rows = offset_ref.shape[0]
    half = mine_ref.shape[1]
    chips = size // 2
    step_rows = rows // pieces
    spans = [(rows, 8)] + [(k * step_rows, step_rows) for k in range(pieces)]
    hops = []
    distance = 1
    while distance < chips:
        hops.append(2 * distance)
        distance *= 2

    def device(q):
        q = lax.rem(q + 2 * size, size)
        return (size - 1 - q if reverse else q,)

    partner = order + 1 - 2 * core
    barrier = pltpu.get_barrier_semaphore()
    targets = [partner] + [order + h for h in hops] + [order - h for h in hops]
    targets += [order + 1, order - 1, order + 2, order - 2]
    for target in targets:
        pl.semaphore_signal(barrier, inc=1, device_id=device(target), device_id_type=MESH)
    pl.semaphore_wait(barrier, len(targets))

    started = []

    def send(src, slot, piece, target):
        first_row, count = spans[piece]
        copy = pltpu.make_async_remote_copy(
            src_ref=src.at[pl.ds(first_row, count), :],
            dst_ref=got.at[slot].at[pl.ds(first_row, count), :],
            send_sem=sends.at[slot, piece],
            recv_sem=recvs.at[slot, piece],
            device_id=device(target),
            device_id_type=MESH,
        )
        copy.start()
        started.append(copy)
        return copy

    first = core == 0
    pending = [send(other_ref, 0, piece, partner) for piece in range(pieces + 1)]
    factor_row = slice(rows, rows + 1)
    for stage in range(len(hops) + 1):
        following = []
        for piece in range(pieces + 1):
            first_row, count = spans[piece]
            part = slice(first_row, first_row + count)
            pending[piece].wait_recv()
            came = got[stage, part, :]
            if stage == 0:
                mine = mine_ref[part, :]
                later = jnp.where(first, came, mine)
                earlier = jnp.where(first, mine, came)
                scale = jnp.where(first, got[0, factor_row, :], mine_ref[factor_row, :])
                if piece == 0:
                    value = later * earlier
                else:
                    value = later + scale * earlier
            else:
                held = total[stage - 1, part, :]
                scale = total[stage - 1, factor_row, :]
                if piece == 0:
                    combined = held * came
                else:
                    combined = held + scale * came
                value = jnp.where(chip >= hops[stage - 1] // 2, combined, held)
            total[stage, part, :] = value
            if stage < len(hops):
                following.append(send(total.at[stage], stage + 1, piece, order + hops[stage]))
        pending = following
    last = len(hops)
    near = [None] + [send(total.at[last], last + 1, piece, order + 1) for piece in range(1, pieces + 1)]
    far = [None] + [send(total.at[last], last + 2, piece, order + 2) for piece in range(1, pieces + 1)]
    early = chip >= 1
    for piece in range(1, pieces + 1):
        first_row, count = spans[piece]
        part = slice(first_row, first_row + count)
        near[piece].wait_recv()
        far[piece].wait_recv()
        close = got[last + 1, part, :]
        own = total[last, part, :]
        before_left = got[last + 2, part, :]
        offset_left = offset_ref[part, :half]
        offset_right = offset_ref[part, half:]
        out_ref[part, :half] = jnp.where(
            first,
            jnp.where(early, offset_left + factor_ref[0:1, :half] * before_left, offset_left),
            close,
        )
        out_ref[part, half:] = jnp.where(
            first,
            jnp.where(early, offset_right + factor_ref[0:1, half:] * close, offset_right),
            own,
        )
    for copy in started:
        copy.wait_send()


def kernel_scan(factor, offset, reverse, ident):
    size, position = (lax.axis_size("depth"), lax.axis_index("depth"))
    rows, width = offset.shape
    half = width // 2
    order = size - 1 - position if reverse else position
    core = order % 2
    spread = jnp.broadcast_to(factor[None, :], (8, width))
    packed = jnp.concatenate([offset, spread], axis=0)
    mine = lax.dynamic_slice_in_dim(packed, core * half, half, axis=1)
    other = lax.dynamic_slice_in_dim(packed, (1 - core) * half, half, axis=1)
    stages = 3 + (size // 2).bit_length() - 1
    return pl.pallas_call(
        functools.partial(scan_kernel, size, reverse, 8),
        out_shape=jax.ShapeDtypeStruct((rows, width), jnp.float32),
        in_specs=[pl.BlockSpec(memory_space=pltpu.VMEM)] * 4,
        out_specs=pl.BlockSpec(memory_space=pltpu.VMEM),
        scratch_shapes=[
            pltpu.VMEM((stages, rows + 8, half), jnp.float32),
            pltpu.VMEM((stages - 2, rows + 8, half), jnp.float32),
            pltpu.SemaphoreType.DMA((stages, 9)),
            pltpu.SemaphoreType.DMA((stages, 9)),
        ],
        compiler_params=pltpu.CompilerParams(collective_id=ident, has_side_effects=True),
    )(mine, other, offset, spread)


def prepare_block(state, w_first, gain_row):
    inverse = lax.rsqrt(jnp.mean(state * state, axis=-1, keepdims=True) + 1e-05)
    normed = (state * inverse * gain_row).astype(jnp.bfloat16)
    preact = jnp.dot(normed, w_first, preferred_element_type=jnp.float32)
    return (inverse, preact)


def finish_block(state, preact, w_second, decay_row):
    hidden = jax.nn.silu(preact).astype(jnp.bfloat16)
    return decay_row * state + jnp.dot(hidden, w_second, preferred_element_type=jnp.float32)


def backward_block(state, inverse, preact, upstream, w_first, w_second, gain_row, decay_row):
    grad_hidden = lax.dot_general(
        upstream.astype(jnp.bfloat16),
        w_second,
        (((1,), (1,)), ((), ())),
        preferred_element_type=jnp.float32,
    )
    sigma = jax.nn.sigmoid(preact)
    grad_pre = (grad_hidden * sigma * (1.0 + preact * (1.0 - sigma))).astype(jnp.bfloat16)
    grad_norm = lax.dot_general(
        grad_pre, w_first, (((1,), (1,)), ((), ())), preferred_element_type=jnp.float32
    )
    scaled = grad_norm * gain_row
    inner = jnp.mean(scaled * state, axis=-1, keepdims=True)
    return decay_row * upstream + inverse * scaled - state * inverse**3 * inner


def relax_forward(start, w_in, w_out, norm_gain, decay, want_end):
    state = start
    count = w_in.shape[0]
    states_list, inverse_list, preact_list = ([], [], [])
    for block in range(count):
        states_list.append(state)
        inverse, preact = prepare_block(state, w_in[block], norm_gain[block])
        inverse_list.append(inverse)
        preact_list.append(preact)
        if want_end or block + 1 < count:
            state = finish_block(state, preact, w_out[block], decay[block])
    return (state, states_list, inverse_list, preact_list)


def relax_backward(start, states, inverses, preacts, w_in, w_out, norm_gain, decay):
    adjoint = start
    count = w_in.shape[0]
    collected = [None] * count
    for block in reversed(range(count)):
        adjoint = backward_block(
            states[block],
            inverses[block],
            preacts[block],
            adjoint,
            w_in[block],
            w_out[block],
            norm_gain[block],
            decay[block],
        )
        collected[block] = adjoint
    return (adjoint, collected)


def compose(earlier, later):
    return (later[0] * earlier[0], later[0] * earlier[1] + later[1])


def shards(state_guess, adjoint_guess, w_in, w_out, norm_gain, decay):
    position = lax.axis_index("depth")
    devices = lax.axis_size("depth")
    factor = jnp.prod(decay, axis=0)
    at_first = position == 0
    at_last = position == devices - 1
    factor_before = shifted(factor, "depth", 1)
    factor_after = shifted(factor, "depth", -1)
    guess_state = state_guess[0]
    end_state, _, _, _ = relax_forward(guess_state, w_in, w_out, norm_gain, decay, True)
    end_before = shifted(end_state, "depth", 1)
    resid = jnp.where(at_first, jnp.zeros_like(guess_state), end_before - guess_state)
    correction = kernel_scan(factor_before, resid, False, 0)
    start = guess_state + correction
    _, states, inverses, preacts = relax_forward(start, w_in, w_out, norm_gain, decay, False)
    guess_adjoint = adjoint_guess[0]
    first_adjoint, _ = relax_backward(
        guess_adjoint, states, inverses, preacts, w_in, w_out, norm_gain, decay
    )
    first_after = shifted(first_adjoint, "depth", -1)
    rho = jnp.where(at_last, jnp.zeros_like(guess_adjoint), first_after - guess_adjoint)
    eps = kernel_scan(factor_after, rho, True, 1)
    head = guess_adjoint + eps
    _, lambdas = relax_backward(head, states, inverses, preacts, w_in, w_out, norm_gain, decay)
    return (jnp.stack(states), jnp.stack(lambdas))


def solution(mesh):
    placed = (
        P("depth", None, None),
        P("depth", None, None),
        P("depth", None, None),
        P("depth", None, None),
        P("depth", None),
        P("depth", None),
    )
    return jax.shard_map(
        shards,
        mesh=mesh,
        in_specs=placed,
        out_specs=(P("depth", None, None), P("depth", None, None)),
        check_vma=False,
    )
```

```python
import functools

import jax
import jax.numpy as jnp
from jax import lax
from jax.experimental import pallas as pl
from jax.experimental.pallas import tpu as pltpu
from jax.sharding import PartitionSpec as P


def shifted(block, axis, distance):
    devices = range(lax.axis_size(axis))
    route = [(i - distance, i) for i in devices if i - distance in devices]
    return lax.ppermute(block, axis, route)


MESH = pl.DeviceIdType.MESH


def group_kernel(size, reverse, pieces, mine_ref, other_ref, offset_ref, factor_ref, out_ref, got, state, q_got, q_state, gathered, full, final, sends, recvs):
    position = lax.axis_index("depth")
    order = size - 1 - position if reverse else position
    core, chip = (order % 2, order // 2)
    ring, group = (chip % 4, chip // 4)
    rows = offset_ref.shape[0]
    half = mine_ref.shape[1]
    groups = size // 8
    quarter = rows // 4
    step_rows = rows // pieces
    spans = [(rows, 8)] + [(k * step_rows, step_rows) for k in range(pieces)]
    spreads = []
    distance = 1
    while distance < groups:
        spreads.append(distance)
        distance *= 2
    depth = len(spreads)
    slot_c, slot_e, slot_f = (3, 4 + depth, 5 + depth)

    def device(q):
        q = lax.rem(q + 2 * size, size)
        return (size - 1 - q if reverse else q,)

    def in_ring(step):
        return order + 2 * ((ring + step + 4) % 4 - ring)

    partner = order + 1 - 2 * core
    source = order - 8 + 2 * (3 - ring)
    sinks = [order + 8 + 2 * (k - 3) for k in range(4)]
    targets = [partner, in_ring(1), in_ring(-1), in_ring(2), in_ring(-2)]
    targets += [order + 8 + 2 * (k - ring) for k in range(4)]
    targets += [order - 8 + 2 * (k - ring) for k in range(4)]
    targets += [order + 8 * s for s in spreads] + [order - 8 * s for s in spreads]
    targets += [in_ring(t) for t in (1, 2, 3)] + [in_ring(-t) for t in (1, 2, 3)]
    targets += [order + 1, order - 1, order + 2, order - 2]
    barrier = pltpu.get_barrier_semaphore()
    for target in targets:
        pl.semaphore_signal(barrier, inc=1, device_id=device(target), device_id_type=MESH)
    last_of_ring = ring == 3
    pl.semaphore_wait(barrier, len(targets))

    started = []

    def copy(src, dst, slot, piece, target, start=True, keep=True, landing=None):
        handle = pltpu.make_async_remote_copy(
            src_ref=src,
            dst_ref=dst,
            send_sem=sends.at[slot, piece],
            recv_sem=recvs.at[slot, piece if landing is None else landing],
            device_id=device(target),
            device_id_type=MESH,
        )
        if start:
            handle.start()
        if start and keep:
            started.append(handle)
        return handle

    def block(ref, piece):
        first_row, count = spans[piece]
        return ref.at[pl.ds(first_row, count), :]

    first = core == 0
    factor_row = slice(rows, rows + 1)
    pending = [copy(block(other_ref, k), block(got.at[0], k), 0, k, partner) for k in range(pieces + 1)]
    for stage in range(3):
        following = []
        for piece in range(pieces + 1):
            first_row, count = spans[piece]
            part = slice(first_row, first_row + count)
            pending[piece].wait_recv()
            came = got[stage, part, :]
            if stage == 0:
                mine = mine_ref[part, :]
                later = jnp.where(first, came, mine)
                earlier = jnp.where(first, mine, came)
                scale = jnp.where(first, got[0, factor_row, :], mine_ref[factor_row, :])
                value = later * earlier if piece == 0 else later + scale * earlier
            else:
                held = state[stage - 1, part, :]
                scale = state[stage - 1, factor_row, :]
                combined = held * came if piece == 0 else held + scale * came
                value = jnp.where(ring >= stage, combined, held)
            state[stage, part, :] = value
            if stage < 2:
                step = 1 if stage == 0 else 2
                following.append(
                    copy(block(state.at[stage], piece), block(got.at[stage + 1], piece), stage + 1, piece, in_ring(step))
                )
        pending = following

    def scatter(start):
        for k in range(4):
            for piece, (first_row, count, landing) in enumerate(((k * quarter, quarter, 0), (rows, 8, quarter))):
                handle = copy(
                    state.at[2].at[pl.ds(first_row, count), :],
                    q_got.at[0].at[pl.ds(landing, count), :],
                    slot_c,
                    2 * k + piece,
                    sinks[k],
                    start=start,
                    keep=False,
                    landing=piece,
                )
                if not start:
                    handle.wait_send()

    @pl.when(last_of_ring)
    def _():
        scatter(True)

    for k, piece_rows in ((0, (0, quarter)), (1, (quarter, 8))):
        copy(
            state.at[2].at[pl.ds(piece_rows[0], piece_rows[1]), :],
            q_got.at[0].at[pl.ds(piece_rows[0], piece_rows[1]), :],
            slot_c,
            k,
            source,
            start=False,
        ).wait_recv()
    incoming = q_got[0]
    is_head = group == 0
    identity = jnp.concatenate(
        [jnp.zeros((quarter, half), jnp.float32), jnp.ones((8, half), jnp.float32)], axis=0
    )
    q_state[0] = jnp.where(is_head, identity, incoming)
    for level, spread in enumerate(spreads):
        copy(q_state.at[level], q_got.at[level + 1], 4 + level, 0, order + 8 * spread).wait_recv()
        held = q_state[level]
        came = q_got[level + 1]
        scale = held[quarter : quarter + 1, :]
        combined = jnp.concatenate([held[:quarter] + scale * came[:quarter], held[quarter:] * came[quarter:]], axis=0)
        q_state[level + 1] = jnp.where(group >= spread, combined, held)
    prefix = q_state.at[depth].at[pl.ds(0, quarter), :]
    spread_copies = [copy(prefix, gathered.at[t - 1], slot_e, t - 1, in_ring(t)) for t in (1, 2, 3)]
    for handle in spread_copies:
        handle.wait_recv()
    scale = state[2, factor_row, :]
    for t in range(4):
        owner = (ring - t + 4) % 4
        band = pl.ds(pl.multiple_of(owner * quarter, quarter), quarter)
        src = q_state[depth, :quarter, :] if t == 0 else gathered[t - 1]
        full[band, :] = state[2, band, :] + scale * src
    near = copy(full, final.at[0], slot_f, 0, order + 1)
    far = copy(full, final.at[1], slot_f, 1, order + 2)
    near.wait_recv()
    far.wait_recv()
    close = final[0]
    own = full[...]
    before_left = final[1]
    offset_left = offset_ref[:, :half]
    offset_right = offset_ref[:, half:]
    early = chip >= 1
    out_ref[:, :half] = jnp.where(
        first,
        jnp.where(early, offset_left + factor_ref[0:1, :half] * before_left, offset_left),
        close,
    )
    out_ref[:, half:] = jnp.where(
        first,
        jnp.where(early, offset_right + factor_ref[0:1, half:] * close, offset_right),
        own,
    )
    for handle in started:
        handle.wait_send()

    @pl.when(last_of_ring)
    def _():
        scatter(False)


def kernel_scan(factor, offset, reverse, ident):
    size, position = (lax.axis_size("depth"), lax.axis_index("depth"))
    rows, width = offset.shape
    half = width // 2
    order = size - 1 - position if reverse else position
    core = order % 2
    spread = jnp.broadcast_to(factor[None, :], (8, width))
    packed = jnp.concatenate([offset, spread], axis=0)
    mine = lax.dynamic_slice_in_dim(packed, core * half, half, axis=1)
    other = lax.dynamic_slice_in_dim(packed, (1 - core) * half, half, axis=1)
    depth = (size // 8).bit_length() - 1
    quarter = rows // 4
    return pl.pallas_call(
        functools.partial(group_kernel, size, reverse, 4),
        out_shape=jax.ShapeDtypeStruct((rows, width), jnp.float32),
        in_specs=[pl.BlockSpec(memory_space=pltpu.VMEM)] * 4,
        out_specs=pl.BlockSpec(memory_space=pltpu.VMEM),
        scratch_shapes=[
            pltpu.VMEM((3, rows + 8, half), jnp.float32),
            pltpu.VMEM((3, rows + 8, half), jnp.float32),
            pltpu.VMEM((depth + 1, quarter + 8, half), jnp.float32),
            pltpu.VMEM((depth + 1, quarter + 8, half), jnp.float32),
            pltpu.VMEM((3, quarter, half), jnp.float32),
            pltpu.VMEM((rows, half), jnp.float32),
            pltpu.VMEM((2, rows, half), jnp.float32),
            pltpu.SemaphoreType.DMA((6 + depth, 8)),
            pltpu.SemaphoreType.DMA((6 + depth, 8)),
        ],
        compiler_params=pltpu.CompilerParams(collective_id=ident, has_side_effects=True),
    )(mine, other, offset, spread)


def prepare_block(state, w_first, gain_row):
    inverse = lax.rsqrt(jnp.mean(state * state, axis=-1, keepdims=True) + 1e-05)
    normed = (state * inverse * gain_row).astype(jnp.bfloat16)
    preact = jnp.dot(normed, w_first, preferred_element_type=jnp.float32)
    return (inverse, preact)


def finish_block(state, preact, w_second, decay_row):
    hidden = jax.nn.silu(preact).astype(jnp.bfloat16)
    return decay_row * state + jnp.dot(hidden, w_second, preferred_element_type=jnp.float32)


def backward_block(state, inverse, preact, upstream, w_first, w_second, gain_row, decay_row):
    grad_hidden = lax.dot_general(
        upstream.astype(jnp.bfloat16),
        w_second,
        (((1,), (1,)), ((), ())),
        preferred_element_type=jnp.float32,
    )
    sigma = jax.nn.sigmoid(preact)
    grad_pre = (grad_hidden * sigma * (1.0 + preact * (1.0 - sigma))).astype(jnp.bfloat16)
    grad_norm = lax.dot_general(
        grad_pre, w_first, (((1,), (1,)), ((), ())), preferred_element_type=jnp.float32
    )
    scaled = grad_norm * gain_row
    inner = jnp.mean(scaled * state, axis=-1, keepdims=True)
    return decay_row * upstream + inverse * scaled - state * inverse**3 * inner


def relax_forward(start, w_in, w_out, norm_gain, decay, want_end):
    state = start
    count = w_in.shape[0]
    states_list, inverse_list, preact_list = ([], [], [])
    for block in range(count):
        states_list.append(state)
        inverse, preact = prepare_block(state, w_in[block], norm_gain[block])
        inverse_list.append(inverse)
        preact_list.append(preact)
        if want_end or block + 1 < count:
            state = finish_block(state, preact, w_out[block], decay[block])
    return (state, states_list, inverse_list, preact_list)


def relax_backward(start, states, inverses, preacts, w_in, w_out, norm_gain, decay):
    adjoint = start
    count = w_in.shape[0]
    collected = [None] * count
    for block in reversed(range(count)):
        adjoint = backward_block(
            states[block],
            inverses[block],
            preacts[block],
            adjoint,
            w_in[block],
            w_out[block],
            norm_gain[block],
            decay[block],
        )
        collected[block] = adjoint
    return (adjoint, collected)


def compose(earlier, later):
    return (later[0] * earlier[0], later[0] * earlier[1] + later[1])


def shards(state_guess, adjoint_guess, w_in, w_out, norm_gain, decay):
    position = lax.axis_index("depth")
    devices = lax.axis_size("depth")
    factor = jnp.prod(decay, axis=0)
    at_first = position == 0
    at_last = position == devices - 1
    factor_before = shifted(factor, "depth", 1)
    factor_after = shifted(factor, "depth", -1)
    guess_state = state_guess[0]
    end_state, _, _, _ = relax_forward(guess_state, w_in, w_out, norm_gain, decay, True)
    end_before = shifted(end_state, "depth", 1)
    resid = jnp.where(at_first, jnp.zeros_like(guess_state), end_before - guess_state)
    correction = kernel_scan(factor_before, resid, False, 0)
    start = guess_state + correction
    _, states, inverses, preacts = relax_forward(start, w_in, w_out, norm_gain, decay, False)
    guess_adjoint = adjoint_guess[0]
    first_adjoint, _ = relax_backward(
        guess_adjoint, states, inverses, preacts, w_in, w_out, norm_gain, decay
    )
    first_after = shifted(first_adjoint, "depth", -1)
    rho = jnp.where(at_last, jnp.zeros_like(guess_adjoint), first_after - guess_adjoint)
    eps = kernel_scan(factor_after, rho, True, 1)
    head = guess_adjoint + eps
    _, lambdas = relax_backward(head, states, inverses, preacts, w_in, w_out, norm_gain, decay)
    return (jnp.stack(states), jnp.stack(lambdas))


def solution(mesh):
    placed = (
        P("depth", None, None),
        P("depth", None, None),
        P("depth", None, None),
        P("depth", None, None),
        P("depth", None),
        P("depth", None),
    )
    return jax.shard_map(
        shards,
        mesh=mesh,
        in_specs=placed,
        out_specs=(P("depth", None, None), P("depth", None, None)),
        check_vma=False,
    )
```

```python
import functools

import jax
import jax.numpy as jnp
from jax import lax
from jax.experimental import pallas as pl
from jax.experimental.pallas import tpu as pltpu
from jax.sharding import PartitionSpec as P


def shifted(block, axis, distance):
    devices = range(lax.axis_size(axis))
    route = [(i - distance, i) for i in devices if i - distance in devices]
    return lax.ppermute(block, axis, route)


MESH = pl.DeviceIdType.MESH


def group_kernel(size, reverse, pieces, mine_ref, other_ref, offset_ref, factor_ref, out_ref, got, state, q_got, q_state, gathered, final, sends, recvs):
    position = lax.axis_index("depth")
    order = size - 1 - position if reverse else position
    core, chip = (order % 2, order // 2)
    ring, group = (chip % 4, chip // 4)
    rows = offset_ref.shape[0]
    half = mine_ref.shape[1]
    groups = size // 8
    quarter = rows // 4
    step_rows = rows // pieces
    spans = [(rows, 8)] + [(k * step_rows, step_rows) for k in range(pieces)]
    levels = []
    width_now = 1
    while width_now < groups:
        ks = [k for k in (1, 2, 3) if k * width_now < groups]
        levels.append((width_now, ks))
        width_now *= len(ks) + 1
    links = [(level, k) for level, (_, ks) in enumerate(levels) for k in ks]
    slot_c, slot_e, slot_f = (3, 4 + len(levels), 5 + len(levels))
    index = order % 8

    def device(q):
        q = lax.rem(q + 2 * size, size)
        return (size - 1 - q if reverse else q,)

    def in_ring(step):
        return order + 2 * ((ring + step + 4) % 4 - ring)

    partner = order + 1 - 2 * core
    source = order - 8 + 2 * (3 - ring)
    sinks = [order + 8 + 2 * (k - 3) for k in range(4)]
    targets = [partner, in_ring(1), in_ring(-1), in_ring(2), in_ring(-2)]
    targets += [order + 8 + 2 * (k - ring) for k in range(4)]
    targets += [order - 8 + 2 * (k - ring) for k in range(4)]
    for spread_width, ks in levels:
        targets += [order + 8 * k * spread_width for k in ks] + [order - 8 * k * spread_width for k in ks]
    targets += [order - index + (index + t) % 8 for t in range(1, 8)]
    targets += [order - index + (index - t + 8) % 8 for t in range(1, 8)]
    targets += [order + 1, order - 1, order + 2, order - 2]
    barrier = pltpu.get_barrier_semaphore()
    for target in targets:
        pl.semaphore_signal(barrier, inc=1, device_id=device(target), device_id_type=MESH)
    last_of_ring = ring == 3
    pl.semaphore_wait(barrier, len(targets))

    started = []

    def copy(src, dst, slot, piece, target, start=True, keep=True, landing=None):
        handle = pltpu.make_async_remote_copy(
            src_ref=src,
            dst_ref=dst,
            send_sem=sends.at[slot, piece],
            recv_sem=recvs.at[slot, piece if landing is None else landing],
            device_id=device(target),
            device_id_type=MESH,
        )
        if start:
            handle.start()
        if start and keep:
            started.append(handle)
        return handle

    def block(ref, piece):
        first_row, count = spans[piece]
        return ref.at[pl.ds(first_row, count), :]

    first = core == 0
    factor_row = slice(rows, rows + 1)
    pending = [copy(block(other_ref, k), block(got.at[0], k), 0, k, partner) for k in range(pieces + 1)]
    for stage in range(3):
        following = []
        for piece in range(pieces + 1):
            first_row, count = spans[piece]
            part = slice(first_row, first_row + count)
            pending[piece].wait_recv()
            came = got[stage, part, :]
            if stage == 0:
                mine = mine_ref[part, :]
                later = jnp.where(first, came, mine)
                earlier = jnp.where(first, mine, came)
                scale = jnp.where(first, got[0, factor_row, :], mine_ref[factor_row, :])
                value = later * earlier if piece == 0 else later + scale * earlier
            else:
                held = state[stage - 1, part, :]
                scale = state[stage - 1, factor_row, :]
                combined = held * came if piece == 0 else held + scale * came
                value = jnp.where(ring >= stage, combined, held)
            state[stage, part, :] = value
            if stage < 2:
                step = 1 if stage == 0 else 2
                following.append(
                    copy(block(state.at[stage], piece), block(got.at[stage + 1], piece), stage + 1, piece, in_ring(step))
                )
        pending = following

    near = copy(state.at[2], final.at[0], slot_f, 0, order + 1)
    far = copy(state.at[2], final.at[1], slot_f, 1, order + 2)

    def scatter(start):
        for k in range(4):
            for piece, (first_row, count, landing) in enumerate(((k * quarter, quarter, 0), (rows, 8, quarter))):
                handle = copy(
                    state.at[2].at[pl.ds(first_row, count), :],
                    q_got.at[0].at[pl.ds(landing, count), :],
                    slot_c,
                    2 * k + piece,
                    sinks[k],
                    start=start,
                    keep=False,
                    landing=piece,
                )
                if not start:
                    handle.wait_send()

    @pl.when(last_of_ring)
    def _():
        scatter(True)

    for k, piece_rows in ((0, (0, quarter)), (1, (quarter, 8))):
        copy(
            state.at[2].at[pl.ds(piece_rows[0], piece_rows[1]), :],
            q_got.at[0].at[pl.ds(piece_rows[0], piece_rows[1]), :],
            slot_c,
            k,
            source,
            start=False,
        ).wait_recv()
    incoming = q_got[0]
    is_head = group == 0
    identity = jnp.concatenate(
        [jnp.zeros((quarter, half), jnp.float32), jnp.ones((8, half), jnp.float32)], axis=0
    )
    q_state[0] = jnp.where(is_head, identity, incoming)
    landing = 1
    for level, (spread_width, ks) in enumerate(levels):
        arrivals = []
        for k in ks:
            arrivals.append((k, copy(q_state.at[level], q_got.at[landing], 4 + level, k - 1, order + 8 * k * spread_width), landing))
            landing += 1
        held = q_state[level]
        for k, handle, spot in arrivals:
            handle.wait_recv()
            came = q_got[spot]
            scale = held[quarter : quarter + 1, :]
            combined = jnp.concatenate([held[:quarter] + scale * came[:quarter], held[quarter:] * came[quarter:]], axis=0)
            held = jnp.where(group >= k * spread_width, combined, held)
        q_state[level + 1] = held
    depth = len(levels)
    prefix = q_state.at[depth].at[pl.ds(0, quarter), :]
    spread_copies = [copy(prefix, gathered.at[t - 1], slot_e, t - 1, order - index + (index + t) % 8) for t in range(1, 8)]
    near.wait_recv()
    far.wait_recv()
    for handle in spread_copies:
        handle.wait_recv()
    at_start = ring == 0
    for t in range(8):
        owner = (index - t + 8) % 8
        owner_ring, owner_core = (owner // 2, owner % 2)
        band = pl.ds(pl.multiple_of(owner_ring * quarter, quarter), quarter)
        cols = pl.ds(pl.multiple_of(owner_core * half, half), half)
        piece = q_state[depth, :quarter, :] if t == 0 else gathered[t - 1]
        left_side = owner_core == 0
        close = final[0, band, :]
        before = jnp.where(left_side, final[1, band, :], close)
        before_scale = jnp.where(left_side, final[1, factor_row, :], final[0, factor_row, :])
        behind = jnp.where(at_start, piece, before + before_scale * piece)
        tail = offset_ref[band, cols] + factor_ref[0:1, cols] * behind
        current = jnp.where(left_side, close, state[2, band, :])
        current_scale = jnp.where(left_side, final[0, factor_row, :], state[2, factor_row, :])
        head = current + current_scale * piece
        out_ref[band, cols] = jnp.where(first, tail, head)
    for handle in started:
        handle.wait_send()

    @pl.when(last_of_ring)
    def _():
        scatter(False)


def kernel_scan(factor, offset, reverse, ident):
    size, position = (lax.axis_size("depth"), lax.axis_index("depth"))
    rows, width = offset.shape
    half = width // 2
    order = size - 1 - position if reverse else position
    core = order % 2
    spread = jnp.broadcast_to(factor[None, :], (8, width))
    packed = jnp.concatenate([offset, spread], axis=0)
    mine = lax.dynamic_slice_in_dim(packed, core * half, half, axis=1)
    other = lax.dynamic_slice_in_dim(packed, (1 - core) * half, half, axis=1)
    groups = size // 8
    links = 0
    levels = 0
    width_now = 1
    while width_now < groups:
        ks = [k for k in (1, 2, 3) if k * width_now < groups]
        links += len(ks)
        levels += 1
        width_now *= len(ks) + 1
    quarter = rows // 4
    return pl.pallas_call(
        functools.partial(group_kernel, size, reverse, 4),
        out_shape=jax.ShapeDtypeStruct((rows, width), jnp.float32),
        in_specs=[pl.BlockSpec(memory_space=pltpu.VMEM)] * 4,
        out_specs=pl.BlockSpec(memory_space=pltpu.VMEM),
        scratch_shapes=[
            pltpu.VMEM((3, rows + 8, half), jnp.float32),
            pltpu.VMEM((3, rows + 8, half), jnp.float32),
            pltpu.VMEM((links + 1, quarter + 8, half), jnp.float32),
            pltpu.VMEM((levels + 1, quarter + 8, half), jnp.float32),
            pltpu.VMEM((7, quarter, half), jnp.float32),
            pltpu.VMEM((2, rows + 8, half), jnp.float32),
            pltpu.SemaphoreType.DMA((6 + levels, 8)),
            pltpu.SemaphoreType.DMA((6 + levels, 8)),
        ],
        compiler_params=pltpu.CompilerParams(collective_id=ident, has_side_effects=True),
    )(mine, other, offset, spread)


def prepare_block(state, w_first, gain_row):
    inverse = lax.rsqrt(jnp.mean(state * state, axis=-1, keepdims=True) + 1e-05)
    normed = (state * inverse * gain_row).astype(jnp.bfloat16)
    preact = jnp.dot(normed, w_first, preferred_element_type=jnp.float32)
    return (inverse, preact)


def finish_block(state, preact, w_second, decay_row):
    hidden = jax.nn.silu(preact).astype(jnp.bfloat16)
    return decay_row * state + jnp.dot(hidden, w_second, preferred_element_type=jnp.float32)


def backward_block(state, inverse, preact, upstream, w_first, w_second, gain_row, decay_row):
    grad_hidden = lax.dot_general(
        upstream.astype(jnp.bfloat16),
        w_second,
        (((1,), (1,)), ((), ())),
        preferred_element_type=jnp.float32,
    )
    sigma = jax.nn.sigmoid(preact)
    grad_pre = (grad_hidden * sigma * (1.0 + preact * (1.0 - sigma))).astype(jnp.bfloat16)
    grad_norm = lax.dot_general(
        grad_pre, w_first, (((1,), (1,)), ((), ())), preferred_element_type=jnp.float32
    )
    scaled = grad_norm * gain_row
    inner = jnp.mean(scaled * state, axis=-1, keepdims=True)
    return decay_row * upstream + inverse * scaled - state * inverse**3 * inner


def relax_forward(start, w_in, w_out, norm_gain, decay, want_end):
    state = start
    count = w_in.shape[0]
    states_list, inverse_list, preact_list = ([], [], [])
    for block in range(count):
        states_list.append(state)
        inverse, preact = prepare_block(state, w_in[block], norm_gain[block])
        inverse_list.append(inverse)
        preact_list.append(preact)
        if want_end or block + 1 < count:
            state = finish_block(state, preact, w_out[block], decay[block])
    return (state, states_list, inverse_list, preact_list)


def relax_backward(start, states, inverses, preacts, w_in, w_out, norm_gain, decay):
    adjoint = start
    count = w_in.shape[0]
    collected = [None] * count
    for block in reversed(range(count)):
        adjoint = backward_block(
            states[block],
            inverses[block],
            preacts[block],
            adjoint,
            w_in[block],
            w_out[block],
            norm_gain[block],
            decay[block],
        )
        collected[block] = adjoint
    return (adjoint, collected)


def compose(earlier, later):
    return (later[0] * earlier[0], later[0] * earlier[1] + later[1])


def shards(state_guess, adjoint_guess, w_in, w_out, norm_gain, decay):
    position = lax.axis_index("depth")
    devices = lax.axis_size("depth")
    factor = jnp.prod(decay, axis=0)
    at_first = position == 0
    at_last = position == devices - 1
    factor_before = shifted(factor, "depth", 1)
    factor_after = shifted(factor, "depth", -1)
    guess_state = state_guess[0]
    end_state, _, _, _ = relax_forward(guess_state, w_in, w_out, norm_gain, decay, True)
    end_before = shifted(end_state, "depth", 1)
    resid = jnp.where(at_first, jnp.zeros_like(guess_state), end_before - guess_state)
    correction = kernel_scan(factor_before, resid, False, 0)
    start = guess_state + correction
    _, states, inverses, preacts = relax_forward(start, w_in, w_out, norm_gain, decay, False)
    guess_adjoint = adjoint_guess[0]
    first_adjoint, _ = relax_backward(
        guess_adjoint, states, inverses, preacts, w_in, w_out, norm_gain, decay
    )
    first_after = shifted(first_adjoint, "depth", -1)
    rho = jnp.where(at_last, jnp.zeros_like(guess_adjoint), first_after - guess_adjoint)
    eps = kernel_scan(factor_after, rho, True, 1)
    head = guess_adjoint + eps
    _, lambdas = relax_backward(head, states, inverses, preacts, w_in, w_out, norm_gain, decay)
    return (jnp.stack(states), jnp.stack(lambdas))


def solution(mesh):
    placed = (
        P("depth", None, None),
        P("depth", None, None),
        P("depth", None, None),
        P("depth", None, None),
        P("depth", None),
        P("depth", None),
    )
    return jax.shard_map(
        shards,
        mesh=mesh,
        in_specs=placed,
        out_specs=(P("depth", None, None), P("depth", None, None)),
        check_vma=False,
    )
```

```python
import functools

import jax
import jax.numpy as jnp
from jax import lax
from jax.experimental import pallas as pl
from jax.experimental.pallas import tpu as pltpu
from jax.sharding import PartitionSpec as P


def shifted(block, axis, distance):
    devices = range(lax.axis_size(axis))
    route = [(i - distance, i) for i in devices if i - distance in devices]
    return lax.ppermute(block, axis, route)


MESH = pl.DeviceIdType.MESH


def group_kernel(size, reverse, pieces, mine_ref, other_ref, out_ref, got, state, q_got, q_state, gathered, final, pair, sends, recvs):
    position = lax.axis_index("depth")
    order = size - 1 - position if reverse else position
    core, chip = (order % 2, order // 2)
    ring, group = (chip % 4, chip // 4)
    rows = out_ref.shape[0]
    half = mine_ref.shape[1]
    groups = size // 8
    quarter = rows // 4
    step_rows = rows // pieces
    spans = [(rows, 8)] + [(k * step_rows, step_rows) for k in range(pieces)]
    levels = []
    width_now = 1
    while width_now < groups:
        ks = [k for k in (1, 2, 3) if k * width_now < groups]
        levels.append((width_now, ks))
        width_now *= len(ks) + 1
    links = [(level, k) for level, (_, ks) in enumerate(levels) for k in ks]
    slot_c, slot_e, slot_f = (3, 4 + len(levels), 5 + len(levels))
    index = order % 8

    def device(q):
        q = lax.rem(q + 2 * size, size)
        return (size - 1 - q if reverse else q,)

    def in_ring(step):
        return order + 2 * ((ring + step + 4) % 4 - ring)

    partner = order + 1 - 2 * core
    source = order - 8 + 2 * (3 - ring)
    sinks = [order + 8 + 2 * (k - 3) for k in range(4)]
    targets = [partner, in_ring(1), in_ring(-1), in_ring(2), in_ring(-2)]
    targets += [order + 8 + 2 * (k - ring) for k in range(4)]
    targets += [order - 8 + 2 * (k - ring) for k in range(4)]
    for spread_width, ks in levels:
        targets += [order + 8 * k * spread_width for k in ks] + [order - 8 * k * spread_width for k in ks]
    targets += [order - index + (index + t) % 8 for t in range(1, 8)]
    targets += [order - index + (index - t + 8) % 8 for t in range(1, 8)]
    targets += [order + 1, order - 1, order + 2, order - 2, order + 3, order - 3]
    barrier = pltpu.get_barrier_semaphore()
    for target in targets:
        pl.semaphore_signal(barrier, inc=1, device_id=device(target), device_id_type=MESH)
    last_of_ring = ring == 3
    pl.semaphore_wait(barrier, len(targets))

    started = []

    def copy(src, dst, slot, piece, target, start=True, keep=True, landing=None):
        handle = pltpu.make_async_remote_copy(
            src_ref=src,
            dst_ref=dst,
            send_sem=sends.at[slot, piece],
            recv_sem=recvs.at[slot, piece if landing is None else landing],
            device_id=device(target),
            device_id_type=MESH,
        )
        if start:
            handle.start()
        if start and keep:
            started.append(handle)
        return handle

    def block(ref, piece):
        first_row, count = spans[piece]
        return ref.at[pl.ds(first_row, count), :]

    first = core == 0
    factor_row = slice(rows, rows + 1)
    pending = [copy(block(other_ref, k), block(got.at[0], k), 0, k, partner) for k in range(pieces + 1)]
    for stage in range(3):
        following = []
        for piece in range(pieces + 1):
            first_row, count = spans[piece]
            part = slice(first_row, first_row + count)
            pending[piece].wait_recv()
            came = got[stage, part, :]
            if stage == 0:
                mine = mine_ref[part, :]
                later = jnp.where(first, came, mine)
                earlier = jnp.where(first, mine, came)
                scale = jnp.where(first, got[0, factor_row, :], mine_ref[factor_row, :])
                value = later * earlier if piece == 0 else later + scale * earlier
            else:
                held = state[stage - 1, part, :]
                scale = state[stage - 1, factor_row, :]
                combined = held * came if piece == 0 else held + scale * came
                value = jnp.where(ring >= stage, combined, held)
            state[stage, part, :] = value
            if stage < 2:
                step = 1 if stage == 0 else 2
                following.append(
                    copy(block(state.at[stage], piece), block(got.at[stage + 1], piece), stage + 1, piece, in_ring(step))
                )
        pending = following

    sides = [copy(state.at[2], final.at[k], slot_f, k, order + 1 + k) for k in range(3)]
    sides.append(copy(mine_ref, pair, slot_f, 3, partner))

    def scatter(start):
        for k in range(4):
            for piece, (first_row, count, landing) in enumerate(((k * quarter, quarter, 0), (rows, 8, quarter))):
                handle = copy(
                    state.at[2].at[pl.ds(first_row, count), :],
                    q_got.at[0].at[pl.ds(landing, count), :],
                    slot_c,
                    2 * k + piece,
                    sinks[k],
                    start=start,
                    keep=False,
                    landing=piece,
                )
                if not start:
                    handle.wait_send()

    @pl.when(last_of_ring)
    def _():
        scatter(True)

    for k, piece_rows in ((0, (0, quarter)), (1, (quarter, 8))):
        copy(
            state.at[2].at[pl.ds(piece_rows[0], piece_rows[1]), :],
            q_got.at[0].at[pl.ds(piece_rows[0], piece_rows[1]), :],
            slot_c,
            k,
            source,
            start=False,
        ).wait_recv()
    incoming = q_got[0]
    is_head = group == 0
    identity = jnp.concatenate(
        [jnp.zeros((quarter, half), jnp.float32), jnp.ones((8, half), jnp.float32)], axis=0
    )
    q_state[0] = jnp.where(is_head, identity, incoming)
    landing = 1
    for level, (spread_width, ks) in enumerate(levels):
        arrivals = []
        for k in ks:
            arrivals.append((k, copy(q_state.at[level], q_got.at[landing], 4 + level, k - 1, order + 8 * k * spread_width), landing))
            landing += 1
        held = q_state[level]
        for k, handle, spot in arrivals:
            handle.wait_recv()
            came = q_got[spot]
            scale = held[quarter : quarter + 1, :]
            combined = jnp.concatenate([held[:quarter] + scale * came[:quarter], held[quarter:] * came[quarter:]], axis=0)
            held = jnp.where(group >= k * spread_width, combined, held)
        q_state[level + 1] = held
    depth = len(levels)
    prefix = q_state.at[depth].at[pl.ds(0, quarter), :]
    spread_copies = [copy(prefix, gathered.at[t - 1], slot_e, t - 1, order - index + (index + t) % 8) for t in range(1, 8)]
    for handle in sides + spread_copies:
        handle.wait_recv()
    at_start = ring == 0
    for t in range(8):
        owner = (index - t + 8) % 8
        owner_ring, owner_core = (owner // 2, owner % 2)
        band = pl.ds(pl.multiple_of(owner_ring * quarter, quarter), quarter)
        piece = q_state[depth, :quarter, :] if t == 0 else gathered[t - 1]
        left_side = owner_core == 0
        low = jnp.where(first, final[1, band, :], final[2, band, :])
        low_scale = jnp.where(first, final[1, factor_row, :], final[2, factor_row, :])
        high = jnp.where(first, final[0, band, :], final[1, band, :])
        high_scale = jnp.where(first, final[0, factor_row, :], final[1, factor_row, :])
        before = jnp.where(left_side, low, high)
        before_scale = jnp.where(left_side, low_scale, high_scale)
        behind = jnp.where(at_start, piece, before + before_scale * piece)
        element = jnp.where(left_side, pair[band, :], got[0, band, :])
        element_scale = jnp.where(left_side, pair[factor_row, :], got[0, factor_row, :])
        cols = pl.ds(pl.multiple_of(owner_core * half, half), half)
        out_ref[band, cols] = jnp.where(first, behind, element + element_scale * behind)
    for handle in started:
        handle.wait_send()

    @pl.when(last_of_ring)
    def _():
        scatter(False)


def kernel_scan(factor, offset, reverse, ident):
    size, position = (lax.axis_size("depth"), lax.axis_index("depth"))
    rows, width = offset.shape
    half = width // 2
    order = size - 1 - position if reverse else position
    core = order % 2
    spread = jnp.broadcast_to(factor[None, :], (8, width))
    packed = jnp.concatenate([offset, spread], axis=0)
    mine = lax.dynamic_slice_in_dim(packed, core * half, half, axis=1)
    other = lax.dynamic_slice_in_dim(packed, (1 - core) * half, half, axis=1)
    groups = size // 8
    links = 0
    levels = 0
    width_now = 1
    while width_now < groups:
        ks = [k for k in (1, 2, 3) if k * width_now < groups]
        links += len(ks)
        levels += 1
        width_now *= len(ks) + 1
    quarter = rows // 4
    return pl.pallas_call(
        functools.partial(group_kernel, size, reverse, 4),
        out_shape=jax.ShapeDtypeStruct((rows, width), jnp.float32),
        in_specs=[pl.BlockSpec(memory_space=pltpu.VMEM)] * 2,
        out_specs=pl.BlockSpec(memory_space=pltpu.VMEM),
        scratch_shapes=[
            pltpu.VMEM((3, rows + 8, half), jnp.float32),
            pltpu.VMEM((3, rows + 8, half), jnp.float32),
            pltpu.VMEM((links + 1, quarter + 8, half), jnp.float32),
            pltpu.VMEM((levels + 1, quarter + 8, half), jnp.float32),
            pltpu.VMEM((7, quarter, half), jnp.float32),
            pltpu.VMEM((3, rows + 8, half), jnp.float32),
            pltpu.VMEM((rows + 8, half), jnp.float32),
            pltpu.SemaphoreType.DMA((6 + levels, 8)),
            pltpu.SemaphoreType.DMA((6 + levels, 8)),
        ],
        compiler_params=pltpu.CompilerParams(collective_id=ident, has_side_effects=True),
    )(mine, other)


def prepare_block(state, w_first, gain_row):
    inverse = lax.rsqrt(jnp.mean(state * state, axis=-1, keepdims=True) + 1e-05)
    normed = (state * inverse * gain_row).astype(jnp.bfloat16)
    preact = jnp.dot(normed, w_first, preferred_element_type=jnp.float32)
    return (inverse, preact)


def finish_block(state, preact, w_second, decay_row):
    hidden = jax.nn.silu(preact).astype(jnp.bfloat16)
    return decay_row * state + jnp.dot(hidden, w_second, preferred_element_type=jnp.float32)


def backward_block(state, inverse, preact, upstream, w_first, w_second, gain_row, decay_row):
    grad_hidden = lax.dot_general(
        upstream.astype(jnp.bfloat16),
        w_second,
        (((1,), (1,)), ((), ())),
        preferred_element_type=jnp.float32,
    )
    sigma = jax.nn.sigmoid(preact)
    grad_pre = (grad_hidden * sigma * (1.0 + preact * (1.0 - sigma))).astype(jnp.bfloat16)
    grad_norm = lax.dot_general(
        grad_pre, w_first, (((1,), (1,)), ((), ())), preferred_element_type=jnp.float32
    )
    scaled = grad_norm * gain_row
    inner = jnp.mean(scaled * state, axis=-1, keepdims=True)
    return decay_row * upstream + inverse * scaled - state * inverse**3 * inner


def relax_forward(start, w_in, w_out, norm_gain, decay, want_end):
    state = start
    count = w_in.shape[0]
    states_list, inverse_list, preact_list = ([], [], [])
    for block in range(count):
        states_list.append(state)
        inverse, preact = prepare_block(state, w_in[block], norm_gain[block])
        inverse_list.append(inverse)
        preact_list.append(preact)
        if want_end or block + 1 < count:
            state = finish_block(state, preact, w_out[block], decay[block])
    return (state, states_list, inverse_list, preact_list)


def relax_backward(start, states, inverses, preacts, w_in, w_out, norm_gain, decay):
    adjoint = start
    count = w_in.shape[0]
    collected = [None] * count
    for block in reversed(range(count)):
        adjoint = backward_block(
            states[block],
            inverses[block],
            preacts[block],
            adjoint,
            w_in[block],
            w_out[block],
            norm_gain[block],
            decay[block],
        )
        collected[block] = adjoint
    return (adjoint, collected)


def compose(earlier, later):
    return (later[0] * earlier[0], later[0] * earlier[1] + later[1])


def shards(state_guess, adjoint_guess, w_in, w_out, norm_gain, decay):
    position = lax.axis_index("depth")
    devices = lax.axis_size("depth")
    factor = jnp.prod(decay, axis=0)
    guess_state = state_guess[0]
    guess_adjoint = adjoint_guess[0]
    next_guess = shifted(guess_state, "depth", -1)
    prev_guess = shifted(guess_adjoint, "depth", 1)
    end_state, _, _, _ = relax_forward(guess_state, w_in, w_out, norm_gain, decay, True)
    correction = kernel_scan(factor, end_state - next_guess, False, 0)
    start = guess_state + correction
    _, states, inverses, preacts = relax_forward(start, w_in, w_out, norm_gain, decay, False)
    first_adjoint, _ = relax_backward(
        guess_adjoint, states, inverses, preacts, w_in, w_out, norm_gain, decay
    )
    eps = kernel_scan(factor, first_adjoint - prev_guess, True, 1)
    head = guess_adjoint + eps
    _, lambdas = relax_backward(head, states, inverses, preacts, w_in, w_out, norm_gain, decay)
    return (jnp.stack(states), jnp.stack(lambdas))


def solution(mesh):
    placed = (
        P("depth", None, None),
        P("depth", None, None),
        P("depth", None, None),
        P("depth", None, None),
        P("depth", None),
        P("depth", None),
    )
    return jax.shard_map(
        shards,
        mesh=mesh,
        in_specs=placed,
        out_specs=(P("depth", None, None), P("depth", None, None)),
        check_vma=False,
    )
```

```python
import functools

import jax
import jax.numpy as jnp
from jax import lax
from jax.experimental import pallas as pl
from jax.experimental.pallas import tpu as pltpu
from jax.sharding import PartitionSpec as P


def shifted(block, axis, distance):
    devices = range(lax.axis_size(axis))
    route = [(i - distance, i) for i in devices if i - distance in devices]
    return lax.ppermute(block, axis, route)


MESH = pl.DeviceIdType.MESH


def radices(groups):
    along_z = min(groups, 8)
    out = []
    for part in (along_z, groups // along_z):
        while part > 1:
            step = 4 if part % 4 == 0 else 2
            out.append(step)
            part //= step
    return out


def group_kernel(size, reverse, pieces, mine_ref, other_ref, out_ref, got, state, q_got, q_state, gathered, final, pair, sends, recvs):
    position = lax.axis_index("depth")
    order = size - 1 - position if reverse else position
    core, chip = (order % 2, order // 2)
    ring, group = (chip % 4, chip // 4)
    rows = out_ref.shape[0]
    half = mine_ref.shape[1]
    groups = size // 8
    quarter = rows // 4
    step_rows = rows // pieces
    spans = [(rows, 8)] + [(k * step_rows, step_rows) for k in range(pieces)]
    levels = []
    width_now = 1
    for step in radices(groups):
        levels.append((width_now, list(range(1, step))))
        width_now *= step
    links = [(level, k) for level, (_, ks) in enumerate(levels) for k in ks]
    slot_c, slot_e, slot_f = (3, 4 + len(levels), 5 + len(levels))
    index = order % 8

    def device(q):
        q = lax.rem(q + 2 * size, size)
        return (size - 1 - q if reverse else q,)

    def in_ring(step):
        return order + 2 * ((ring + step + 4) % 4 - ring)

    partner = order + 1 - 2 * core
    source = order - 8 + 2 * (3 - ring)
    sinks = [order + 8 + 2 * (k - 3) for k in range(4)]
    targets = [order + 8 + 2 * (k - ring) for k in range(4)]
    targets += [order - 8 + 2 * (k - ring) for k in range(4)]
    for spread_width, ks in levels:
        targets += [order + 8 * k * spread_width for k in ks] + [order - 8 * k * spread_width for k in ks]
    targets += [order - index + (index + t) % 8 for t in range(1, 8)]
    targets += [order + 1, order - 1, order + 2, order - 2, order + 3, order - 3]
    barrier = pltpu.get_barrier_semaphore()
    for target in targets:
        pl.semaphore_signal(barrier, inc=1, device_id=device(target), device_id_type=MESH)
    last_of_ring = ring == 3
    pl.semaphore_wait(barrier, len(targets))

    started = []

    def copy(src, dst, slot, piece, target, start=True, keep=True, landing=None):
        handle = pltpu.make_async_remote_copy(
            src_ref=src,
            dst_ref=dst,
            send_sem=sends.at[slot, piece],
            recv_sem=recvs.at[slot, piece if landing is None else landing],
            device_id=device(target),
            device_id_type=MESH,
        )
        if start:
            handle.start()
        if start and keep:
            started.append(handle)
        return handle

    def block(ref, piece):
        first_row, count = spans[piece]
        return ref.at[pl.ds(first_row, count), :]

    first = core == 0
    factor_row = slice(rows, rows + 1)
    pending = [copy(block(other_ref, k), block(got.at[0], k), 0, k, partner) for k in range(pieces + 1)]
    for stage in range(3):
        following = []
        for piece in range(pieces + 1):
            first_row, count = spans[piece]
            part = slice(first_row, first_row + count)
            pending[piece].wait_recv()
            came = got[stage, part, :]
            if stage == 0:
                mine = mine_ref[part, :]
                later = jnp.where(first, came, mine)
                earlier = jnp.where(first, mine, came)
                scale = jnp.where(first, got[0, factor_row, :], mine_ref[factor_row, :])
                value = later * earlier if piece == 0 else later + scale * earlier
            else:
                held = state[stage - 1, part, :]
                scale = state[stage - 1, factor_row, :]
                combined = held * came if piece == 0 else held + scale * came
                value = jnp.where(ring >= stage, combined, held)
            state[stage, part, :] = value
            if stage < 2:
                step = 1 if stage == 0 else 2
                following.append(
                    copy(block(state.at[stage], piece), block(got.at[stage + 1], piece), stage + 1, piece, in_ring(step))
                )
        pending = following

    sides = [copy(state.at[2], final.at[k], slot_f, k, order + 1 + k) for k in range(3)]
    sides.append(copy(mine_ref, pair, slot_f, 3, partner))

    def scatter(start):
        for k in range(4):
            for piece, (first_row, count, landing) in enumerate(((k * quarter, quarter, 0), (rows, 8, quarter))):
                handle = copy(
                    state.at[2].at[pl.ds(first_row, count), :],
                    q_got.at[0].at[pl.ds(landing, count), :],
                    slot_c,
                    2 * k + piece,
                    sinks[k],
                    start=start,
                    keep=False,
                    landing=piece,
                )
                if not start:
                    handle.wait_send()

    @pl.when(last_of_ring)
    def _():
        scatter(True)

    for k, piece_rows in ((0, (0, quarter)), (1, (quarter, 8))):
        copy(
            state.at[2].at[pl.ds(piece_rows[0], piece_rows[1]), :],
            q_got.at[0].at[pl.ds(piece_rows[0], piece_rows[1]), :],
            slot_c,
            k,
            source,
            start=False,
        ).wait_recv()
    incoming = q_got[0]
    is_head = group == 0
    identity = jnp.concatenate(
        [jnp.zeros((quarter, half), jnp.float32), jnp.ones((8, half), jnp.float32)], axis=0
    )
    q_state[0] = jnp.where(is_head, identity, incoming)
    landing = 1
    for level, (spread_width, ks) in enumerate(levels):
        arrivals = []
        for k in ks:
            arrivals.append((k, copy(q_state.at[level], q_got.at[landing], 4 + level, k - 1, order + 8 * k * spread_width), landing))
            landing += 1
        held = q_state[level]
        for k, handle, spot in arrivals:
            handle.wait_recv()
            came = q_got[spot]
            scale = held[quarter : quarter + 1, :]
            combined = jnp.concatenate([held[:quarter] + scale * came[:quarter], held[quarter:] * came[quarter:]], axis=0)
            held = jnp.where(group >= k * spread_width, combined, held)
        q_state[level + 1] = held
    depth = len(levels)
    prefix = q_state.at[depth].at[pl.ds(0, quarter), :]
    spread_copies = [copy(prefix, gathered.at[t - 1], slot_e, t - 1, order - index + (index + t) % 8) for t in range(1, 8)]
    for handle in sides + spread_copies:
        handle.wait_recv()
    at_start = ring == 0
    for t in range(8):
        owner = (index - t + 8) % 8
        owner_ring, owner_core = (owner // 2, owner % 2)
        band = pl.ds(pl.multiple_of(owner_ring * quarter, quarter), quarter)
        piece = q_state[depth, :quarter, :] if t == 0 else gathered[t - 1]
        left_side = owner_core == 0
        low = jnp.where(first, final[1, band, :], final[2, band, :])
        low_scale = jnp.where(first, final[1, factor_row, :], final[2, factor_row, :])
        high = jnp.where(first, final[0, band, :], final[1, band, :])
        high_scale = jnp.where(first, final[0, factor_row, :], final[1, factor_row, :])
        before = jnp.where(left_side, low, high)
        before_scale = jnp.where(left_side, low_scale, high_scale)
        behind = jnp.where(at_start, piece, before + before_scale * piece)
        element = jnp.where(left_side, pair[band, :], got[0, band, :])
        element_scale = jnp.where(left_side, pair[factor_row, :], got[0, factor_row, :])
        cols = pl.ds(pl.multiple_of(owner_core * half, half), half)
        out_ref[band, cols] = jnp.where(first, behind, element + element_scale * behind)
    for handle in started:
        handle.wait_send()

    @pl.when(last_of_ring)
    def _():
        scatter(False)


def kernel_scan(factor, offset, reverse, ident):
    size, position = (lax.axis_size("depth"), lax.axis_index("depth"))
    rows, width = offset.shape
    half = width // 2
    order = size - 1 - position if reverse else position
    core = order % 2
    spread = jnp.broadcast_to(factor[None, :], (8, width))
    packed = jnp.concatenate([offset, spread], axis=0)
    mine = lax.dynamic_slice_in_dim(packed, core * half, half, axis=1)
    other = lax.dynamic_slice_in_dim(packed, (1 - core) * half, half, axis=1)
    groups = size // 8
    links = sum(step - 1 for step in radices(groups))
    levels = len(radices(groups))
    quarter = rows // 4
    return pl.pallas_call(
        functools.partial(group_kernel, size, reverse, 4),
        out_shape=jax.ShapeDtypeStruct((rows, width), jnp.float32),
        in_specs=[pl.BlockSpec(memory_space=pltpu.VMEM)] * 2,
        out_specs=pl.BlockSpec(memory_space=pltpu.VMEM),
        scratch_shapes=[
            pltpu.VMEM((3, rows + 8, half), jnp.float32),
            pltpu.VMEM((3, rows + 8, half), jnp.float32),
            pltpu.VMEM((links + 1, quarter + 8, half), jnp.float32),
            pltpu.VMEM((levels + 1, quarter + 8, half), jnp.float32),
            pltpu.VMEM((7, quarter, half), jnp.float32),
            pltpu.VMEM((3, rows + 8, half), jnp.float32),
            pltpu.VMEM((rows + 8, half), jnp.float32),
            pltpu.SemaphoreType.DMA((6 + levels, 8)),
            pltpu.SemaphoreType.DMA((6 + levels, 8)),
        ],
        compiler_params=pltpu.CompilerParams(collective_id=ident, has_side_effects=True),
    )(mine, other)


def prepare_block(state, w_first, gain_row):
    inverse = lax.rsqrt(jnp.mean(state * state, axis=-1, keepdims=True) + 1e-05)
    normed = (state * inverse * gain_row).astype(jnp.bfloat16)
    preact = jnp.dot(normed, w_first, preferred_element_type=jnp.float32)
    return (inverse, preact)


def finish_block(state, preact, w_second, decay_row):
    hidden = jax.nn.silu(preact).astype(jnp.bfloat16)
    return decay_row * state + jnp.dot(hidden, w_second, preferred_element_type=jnp.float32)


def backward_block(state, inverse, preact, upstream, w_first, w_second, gain_row, decay_row):
    grad_hidden = lax.dot_general(
        upstream.astype(jnp.bfloat16),
        w_second,
        (((1,), (1,)), ((), ())),
        preferred_element_type=jnp.float32,
    )
    sigma = jax.nn.sigmoid(preact)
    grad_pre = (grad_hidden * sigma * (1.0 + preact * (1.0 - sigma))).astype(jnp.bfloat16)
    grad_norm = lax.dot_general(
        grad_pre, w_first, (((1,), (1,)), ((), ())), preferred_element_type=jnp.float32
    )
    scaled = grad_norm * gain_row
    inner = jnp.mean(scaled * state, axis=-1, keepdims=True)
    return decay_row * upstream + inverse * scaled - state * inverse**3 * inner


def relax_forward(start, w_in, w_out, norm_gain, decay, want_end):
    state = start
    count = w_in.shape[0]
    states_list, inverse_list, preact_list = ([], [], [])
    for block in range(count):
        states_list.append(state)
        inverse, preact = prepare_block(state, w_in[block], norm_gain[block])
        inverse_list.append(inverse)
        preact_list.append(preact)
        if want_end or block + 1 < count:
            state = finish_block(state, preact, w_out[block], decay[block])
    return (state, states_list, inverse_list, preact_list)


def relax_backward(start, states, inverses, preacts, w_in, w_out, norm_gain, decay):
    adjoint = start
    count = w_in.shape[0]
    collected = [None] * count
    for block in reversed(range(count)):
        adjoint = backward_block(
            states[block],
            inverses[block],
            preacts[block],
            adjoint,
            w_in[block],
            w_out[block],
            norm_gain[block],
            decay[block],
        )
        collected[block] = adjoint
    return (adjoint, collected)


def compose(earlier, later):
    return (later[0] * earlier[0], later[0] * earlier[1] + later[1])


def shards(state_guess, adjoint_guess, w_in, w_out, norm_gain, decay):
    position = lax.axis_index("depth")
    devices = lax.axis_size("depth")
    factor = jnp.prod(decay, axis=0)
    guess_state = state_guess[0]
    guess_adjoint = adjoint_guess[0]
    next_guess = shifted(guess_state, "depth", -1)
    prev_guess = shifted(guess_adjoint, "depth", 1)
    end_state, _, _, _ = relax_forward(guess_state, w_in, w_out, norm_gain, decay, True)
    correction = kernel_scan(factor, end_state - next_guess, False, 0)
    start = guess_state + correction
    _, states, inverses, preacts = relax_forward(start, w_in, w_out, norm_gain, decay, False)
    first_adjoint, _ = relax_backward(
        guess_adjoint, states, inverses, preacts, w_in, w_out, norm_gain, decay
    )
    eps = kernel_scan(factor, first_adjoint - prev_guess, True, 1)
    head = guess_adjoint + eps
    _, lambdas = relax_backward(head, states, inverses, preacts, w_in, w_out, norm_gain, decay)
    return (jnp.stack(states), jnp.stack(lambdas))


def solution(mesh):
    placed = (
        P("depth", None, None),
        P("depth", None, None),
        P("depth", None, None),
        P("depth", None, None),
        P("depth", None),
        P("depth", None),
    )
    return jax.shard_map(
        shards,
        mesh=mesh,
        in_specs=placed,
        out_specs=(P("depth", None, None), P("depth", None, None)),
        check_vma=False,
    )
```

```python
import functools

import jax
import jax.numpy as jnp
from jax import lax
from jax.experimental import pallas as pl
from jax.experimental.pallas import tpu as pltpu
from jax.sharding import PartitionSpec as P


def shifted(block, axis, distance):
    devices = range(lax.axis_size(axis))
    route = [(i - distance, i) for i in devices if i - distance in devices]
    return lax.ppermute(block, axis, route)


MESH = pl.DeviceIdType.MESH


def radices(groups):
    along_z = min(groups, 8)
    out = []
    for part in (along_z, groups // along_z):
        while part > 1:
            step = 4 if part % 4 == 0 else 2
            out.append(step)
            part //= step
    return out


def group_kernel(size, reverse, pieces, packed_ref, out_ref, got, state, q_got, q_state, gathered, final, pair, sends, recvs):
    position = lax.axis_index("depth")
    order = size - 1 - position if reverse else position
    core, chip = (order % 2, order // 2)
    ring, group = (chip % 4, chip // 4)
    rows = out_ref.shape[0]
    half = packed_ref.shape[1] // 2
    groups = size // 8
    quarter = rows // 4
    step_rows = rows // pieces
    spans = [(rows, 8)] + [(k * step_rows, step_rows) for k in range(pieces)]
    levels = []
    width_now = 1
    for step in radices(groups):
        levels.append((width_now, list(range(1, step))))
        width_now *= step
    links = [(level, k) for level, (_, ks) in enumerate(levels) for k in ks]
    slot_c, slot_e, slot_f = (3, 4 + len(levels), 5 + len(levels))
    index = order % 8

    def device(q):
        q = lax.rem(q + 2 * size, size)
        return (size - 1 - q if reverse else q,)

    def in_ring(step):
        return order + 2 * ((ring + step + 4) % 4 - ring)

    partner = order + 1 - 2 * core
    source = order - 8 + 2 * (3 - ring)
    sinks = [order + 8 + 2 * (k - 3) for k in range(4)]
    targets = [order + 8 + 2 * (k - ring) for k in range(4)]
    targets += [order - 8 + 2 * (k - ring) for k in range(4)]
    for spread_width, ks in levels:
        targets += [order + 8 * k * spread_width for k in ks] + [order - 8 * k * spread_width for k in ks]
    targets += [order - index + (index + t) % 8 for t in range(1, 8)]
    targets += [order + 1, order - 1, order + 2, order - 2, order + 3, order - 3]
    barrier = pltpu.get_barrier_semaphore()
    for target in targets:
        pl.semaphore_signal(barrier, inc=1, device_id=device(target), device_id_type=MESH)
    last_of_ring = ring == 3
    pl.semaphore_wait(barrier, len(targets))

    started = []

    def copy(src, dst, slot, piece, target, start=True, keep=True, landing=None):
        handle = pltpu.make_async_remote_copy(
            src_ref=src,
            dst_ref=dst,
            send_sem=sends.at[slot, piece],
            recv_sem=recvs.at[slot, piece if landing is None else landing],
            device_id=device(target),
            device_id_type=MESH,
        )
        if start:
            handle.start()
        if start and keep:
            started.append(handle)
        return handle

    def block(ref, piece):
        first_row, count = spans[piece]
        return ref.at[pl.ds(first_row, count), :]

    first = core == 0
    factor_row = slice(rows, rows + 1)
    mine_ref = packed_ref.at[:, pl.ds(pl.multiple_of(core * half, half), half)]
    other_ref = packed_ref.at[:, pl.ds(pl.multiple_of((1 - core) * half, half), half)]
    pending = [copy(block(other_ref, k), block(got.at[0], k), 0, k, partner) for k in range(pieces + 1)]
    for stage in range(3):
        following = []
        for piece in range(pieces + 1):
            first_row, count = spans[piece]
            part = slice(first_row, first_row + count)
            pending[piece].wait_recv()
            came = got[stage, part, :]
            if stage == 0:
                mine = mine_ref[part, :]
                later = jnp.where(first, came, mine)
                earlier = jnp.where(first, mine, came)
                scale = jnp.where(first, got[0, factor_row, :], mine_ref[factor_row, :])
                value = later * earlier if piece == 0 else later + scale * earlier
            else:
                held = state[stage - 1, part, :]
                scale = state[stage - 1, factor_row, :]
                combined = held * came if piece == 0 else held + scale * came
                value = jnp.where(ring >= stage, combined, held)
            state[stage, part, :] = value
            if stage < 2:
                step = 1 if stage == 0 else 2
                following.append(
                    copy(block(state.at[stage], piece), block(got.at[stage + 1], piece), stage + 1, piece, in_ring(step))
                )
        pending = following

    sides = [copy(state.at[2], final.at[k], slot_f, k, order + 1 + k) for k in range(3)]
    sides.append(copy(mine_ref, pair, slot_f, 3, partner))

    def scatter(start):
        for k in range(4):
            for piece, (first_row, count, landing) in enumerate(((k * quarter, quarter, 0), (rows, 8, quarter))):
                handle = copy(
                    state.at[2].at[pl.ds(first_row, count), :],
                    q_got.at[0].at[pl.ds(landing, count), :],
                    slot_c,
                    2 * k + piece,
                    sinks[k],
                    start=start,
                    keep=False,
                    landing=piece,
                )
                if not start:
                    handle.wait_send()

    @pl.when(last_of_ring)
    def _():
        scatter(True)

    for k, piece_rows in ((0, (0, quarter)), (1, (quarter, 8))):
        copy(
            state.at[2].at[pl.ds(piece_rows[0], piece_rows[1]), :],
            q_got.at[0].at[pl.ds(piece_rows[0], piece_rows[1]), :],
            slot_c,
            k,
            source,
            start=False,
        ).wait_recv()
    incoming = q_got[0]
    is_head = group == 0
    identity = jnp.concatenate(
        [jnp.zeros((quarter, half), jnp.float32), jnp.ones((8, half), jnp.float32)], axis=0
    )
    q_state[0] = jnp.where(is_head, identity, incoming)
    landing = 1
    for level, (spread_width, ks) in enumerate(levels):
        arrivals = []
        for k in ks:
            arrivals.append((k, copy(q_state.at[level], q_got.at[landing], 4 + level, k - 1, order + 8 * k * spread_width), landing))
            landing += 1
        held = q_state[level]
        for k, handle, spot in arrivals:
            handle.wait_recv()
            came = q_got[spot]
            scale = held[quarter : quarter + 1, :]
            combined = jnp.concatenate([held[:quarter] + scale * came[:quarter], held[quarter:] * came[quarter:]], axis=0)
            held = jnp.where(group >= k * spread_width, combined, held)
        q_state[level + 1] = held
    depth = len(levels)
    prefix = q_state.at[depth].at[pl.ds(0, quarter), :]
    spread_copies = [copy(prefix, gathered.at[t - 1], slot_e, t - 1, order - index + (index + t) % 8) for t in range(1, 8)]
    for handle in sides + spread_copies:
        handle.wait_recv()
    at_start = ring == 0
    for t in range(8):
        owner = (index - t + 8) % 8
        owner_ring, owner_core = (owner // 2, owner % 2)
        band = pl.ds(pl.multiple_of(owner_ring * quarter, quarter), quarter)
        piece = q_state[depth, :quarter, :] if t == 0 else gathered[t - 1]
        left_side = owner_core == 0
        low = jnp.where(first, final[1, band, :], final[2, band, :])
        low_scale = jnp.where(first, final[1, factor_row, :], final[2, factor_row, :])
        high = jnp.where(first, final[0, band, :], final[1, band, :])
        high_scale = jnp.where(first, final[0, factor_row, :], final[1, factor_row, :])
        before = jnp.where(left_side, low, high)
        before_scale = jnp.where(left_side, low_scale, high_scale)
        behind = jnp.where(at_start, piece, before + before_scale * piece)
        element = jnp.where(left_side, pair[band, :], got[0, band, :])
        element_scale = jnp.where(left_side, pair[factor_row, :], got[0, factor_row, :])
        cols = pl.ds(pl.multiple_of(owner_core * half, half), half)
        out_ref[band, cols] = jnp.where(first, behind, element + element_scale * behind)
    for handle in started:
        handle.wait_send()

    @pl.when(last_of_ring)
    def _():
        scatter(False)


def kernel_scan(factor, offset, reverse, ident):
    size = lax.axis_size("depth")
    rows, width = offset.shape
    half = width // 2
    spread = jnp.broadcast_to(factor[None, :], (8, width))
    packed = jnp.concatenate([offset, spread], axis=0)
    groups = size // 8
    links = sum(step - 1 for step in radices(groups))
    levels = len(radices(groups))
    quarter = rows // 4
    return pl.pallas_call(
        functools.partial(group_kernel, size, reverse, 4),
        out_shape=jax.ShapeDtypeStruct((rows, width), jnp.float32),
        in_specs=[pl.BlockSpec(memory_space=pltpu.VMEM)],
        out_specs=pl.BlockSpec(memory_space=pltpu.VMEM),
        scratch_shapes=[
            pltpu.VMEM((3, rows + 8, half), jnp.float32),
            pltpu.VMEM((3, rows + 8, half), jnp.float32),
            pltpu.VMEM((links + 1, quarter + 8, half), jnp.float32),
            pltpu.VMEM((levels + 1, quarter + 8, half), jnp.float32),
            pltpu.VMEM((7, quarter, half), jnp.float32),
            pltpu.VMEM((3, rows + 8, half), jnp.float32),
            pltpu.VMEM((rows + 8, half), jnp.float32),
            pltpu.SemaphoreType.DMA((6 + levels, 8)),
            pltpu.SemaphoreType.DMA((6 + levels, 8)),
        ],
        compiler_params=pltpu.CompilerParams(collective_id=ident, has_side_effects=True),
    )(packed)


def prepare_block(state, w_first, gain_row):
    inverse = lax.rsqrt(jnp.mean(state * state, axis=-1, keepdims=True) + 1e-05)
    normed = (state * inverse * gain_row).astype(jnp.bfloat16)
    preact = jnp.dot(normed, w_first, preferred_element_type=jnp.float32)
    return (inverse, preact)


def finish_block(state, preact, w_second, decay_row):
    hidden = jax.nn.silu(preact).astype(jnp.bfloat16)
    return decay_row * state + jnp.dot(hidden, w_second, preferred_element_type=jnp.float32)


def backward_block(state, inverse, preact, upstream, w_first, w_second, gain_row, decay_row):
    grad_hidden = lax.dot_general(
        upstream.astype(jnp.bfloat16),
        w_second,
        (((1,), (1,)), ((), ())),
        preferred_element_type=jnp.float32,
    )
    sigma = jax.nn.sigmoid(preact)
    grad_pre = (grad_hidden * sigma * (1.0 + preact * (1.0 - sigma))).astype(jnp.bfloat16)
    grad_norm = lax.dot_general(
        grad_pre, w_first, (((1,), (1,)), ((), ())), preferred_element_type=jnp.float32
    )
    scaled = grad_norm * gain_row
    inner = jnp.mean(scaled * state, axis=-1, keepdims=True)
    return decay_row * upstream + inverse * scaled - state * inverse**3 * inner


def relax_forward(start, w_in, w_out, norm_gain, decay, want_end):
    state = start
    count = w_in.shape[0]
    states_list, inverse_list, preact_list = ([], [], [])
    for block in range(count):
        states_list.append(state)
        inverse, preact = prepare_block(state, w_in[block], norm_gain[block])
        inverse_list.append(inverse)
        preact_list.append(preact)
        if want_end or block + 1 < count:
            state = finish_block(state, preact, w_out[block], decay[block])
    return (state, states_list, inverse_list, preact_list)


def relax_backward(start, states, inverses, preacts, w_in, w_out, norm_gain, decay):
    adjoint = start
    count = w_in.shape[0]
    collected = [None] * count
    for block in reversed(range(count)):
        adjoint = backward_block(
            states[block],
            inverses[block],
            preacts[block],
            adjoint,
            w_in[block],
            w_out[block],
            norm_gain[block],
            decay[block],
        )
        collected[block] = adjoint
    return (adjoint, collected)


def compose(earlier, later):
    return (later[0] * earlier[0], later[0] * earlier[1] + later[1])


def shards(state_guess, adjoint_guess, w_in, w_out, norm_gain, decay):
    factor = jnp.prod(decay, axis=0)
    guess_state = state_guess[0]
    guess_adjoint = adjoint_guess[0]
    next_guess = shifted(guess_state, "depth", -1)
    prev_guess = shifted(guess_adjoint, "depth", 1)
    end_state, _, _, _ = relax_forward(guess_state, w_in, w_out, norm_gain, decay, True)
    correction = kernel_scan(factor, end_state - next_guess, False, 0)
    start = guess_state + correction
    _, states, inverses, preacts = relax_forward(start, w_in, w_out, norm_gain, decay, False)
    first_adjoint, _ = relax_backward(
        guess_adjoint, states, inverses, preacts, w_in, w_out, norm_gain, decay
    )
    eps = kernel_scan(factor, first_adjoint - prev_guess, True, 1)
    head = guess_adjoint + eps
    _, lambdas = relax_backward(head, states, inverses, preacts, w_in, w_out, norm_gain, decay)
    return (jnp.stack(states), jnp.stack(lambdas))


def solution(mesh):
    placed = (
        P("depth", None, None),
        P("depth", None, None),
        P("depth", None, None),
        P("depth", None, None),
        P("depth", None),
        P("depth", None),
    )
    return jax.shard_map(
        shards,
        mesh=mesh,
        in_specs=placed,
        out_specs=(P("depth", None, None), P("depth", None, None)),
        check_vma=False,
    )
```

```python
import functools

import jax
import jax.numpy as jnp
from jax import lax
from jax.experimental import pallas as pl
from jax.experimental.pallas import tpu as pltpu
from jax.sharding import PartitionSpec as P


def shifted(block, axis, distance):
    devices = range(lax.axis_size(axis))
    route = [(i - distance, i) for i in devices if i - distance in devices]
    return lax.ppermute(block, axis, route)


MESH = pl.DeviceIdType.MESH


def radices(groups):
    along_z = min(groups, 8)
    out = []
    for part in (along_z, groups // along_z):
        while part > 1:
            step = 4 if part % 4 == 0 else 2
            out.append(step)
            part //= step
    return out


def group_kernel(size, reverse, pieces, carry, *refs):
    if carry:
        packed_ref, carry_ref, out_ref, carry_out, got, state, q_got, q_state, gathered, final, pair, held_carry, sends, recvs = refs
    else:
        packed_ref, out_ref, got, state, q_got, q_state, gathered, final, pair, sends, recvs = refs
    position = lax.axis_index("depth")
    order = size - 1 - position if reverse else position
    core, chip = (order % 2, order // 2)
    ring, group = (chip % 4, chip // 4)
    rows = out_ref.shape[0]
    half = packed_ref.shape[1] // 2
    groups = size // 8
    quarter = rows // 4
    step_rows = rows // pieces
    spans = [(rows, 8)] + [(k * step_rows, step_rows) for k in range(pieces)]
    levels = []
    width_now = 1
    for step in radices(groups):
        levels.append((width_now, list(range(1, step))))
        width_now *= step
    links = [(level, k) for level, (_, ks) in enumerate(levels) for k in ks]
    slot_c, slot_e, slot_f = (3, 4 + len(levels), 5 + len(levels))
    index = order % 8

    def device(q):
        q = lax.rem(q + 2 * size, size)
        return (size - 1 - q if reverse else q,)

    def in_ring(step):
        return order + 2 * ((ring + step + 4) % 4 - ring)

    partner = order + 1 - 2 * core
    source = order - 8 + 2 * (3 - ring)
    sinks = [order + 8 + 2 * (k - 3) for k in range(4)]
    targets = [order + 8 + 2 * (k - ring) for k in range(4)]
    targets += [order - 8 + 2 * (k - ring) for k in range(4)]
    for spread_width, ks in levels:
        targets += [order + 8 * k * spread_width for k in ks] + [order - 8 * k * spread_width for k in ks]
    targets += [order - index + (index + t) % 8 for t in range(1, 8)]
    targets += [order + 1, order - 1, order + 2, order - 2, order + 3, order - 3]
    barrier = pltpu.get_barrier_semaphore()
    for target in targets:
        pl.semaphore_signal(barrier, inc=1, device_id=device(target), device_id_type=MESH)
    last_of_ring = ring == 3
    pl.semaphore_wait(barrier, len(targets))

    started = []

    def copy(src, dst, slot, piece, target, start=True, keep=True, landing=None):
        handle = pltpu.make_async_remote_copy(
            src_ref=src,
            dst_ref=dst,
            send_sem=sends.at[slot, piece],
            recv_sem=recvs.at[slot, piece if landing is None else landing],
            device_id=device(target),
            device_id_type=MESH,
        )
        if start:
            handle.start()
        if start and keep:
            started.append(handle)
        return handle

    def block(ref, piece):
        first_row, count = spans[piece]
        return ref.at[pl.ds(first_row, count), :]

    first = core == 0
    factor_row = slice(rows, rows + 1)
    mine_ref = packed_ref.at[:, pl.ds(pl.multiple_of(core * half, half), half)]
    other_ref = packed_ref.at[:, pl.ds(pl.multiple_of((1 - core) * half, half), half)]
    pending = [copy(block(other_ref, k), block(got.at[0], k), 0, k, partner) for k in range(pieces + 1)]
    for stage in range(3):
        following = []
        for piece in range(pieces + 1):
            first_row, count = spans[piece]
            part = slice(first_row, first_row + count)
            pending[piece].wait_recv()
            came = got[stage, part, :]
            if stage == 0:
                mine = mine_ref[part, :]
                later = jnp.where(first, came, mine)
                earlier = jnp.where(first, mine, came)
                scale = jnp.where(first, got[0, factor_row, :], mine_ref[factor_row, :])
                value = later * earlier if piece == 0 else later + scale * earlier
            else:
                held = state[stage - 1, part, :]
                scale = state[stage - 1, factor_row, :]
                combined = held * came if piece == 0 else held + scale * came
                value = jnp.where(ring >= stage, combined, held)
            state[stage, part, :] = value
            if stage < 2:
                step = 1 if stage == 0 else 2
                following.append(
                    copy(block(state.at[stage], piece), block(got.at[stage + 1], piece), stage + 1, piece, in_ring(step))
                )
        pending = following

    sides = [copy(state.at[2], final.at[k], slot_f, k, order + 1 + k) for k in range(3)]
    sides.append(copy(mine_ref, pair, slot_f, 3, partner))
    if carry:
        sides.append(copy(carry_ref, held_carry, slot_f, 4, order + 1))

    def scatter(start):
        for k in range(4):
            for piece, (first_row, count, landing) in enumerate(((k * quarter, quarter, 0), (rows, 8, quarter))):
                handle = copy(
                    state.at[2].at[pl.ds(first_row, count), :],
                    q_got.at[0].at[pl.ds(landing, count), :],
                    slot_c,
                    2 * k + piece,
                    sinks[k],
                    start=start,
                    keep=False,
                    landing=piece,
                )
                if not start:
                    handle.wait_send()

    @pl.when(last_of_ring)
    def _():
        scatter(True)

    for k, piece_rows in ((0, (0, quarter)), (1, (quarter, 8))):
        copy(
            state.at[2].at[pl.ds(piece_rows[0], piece_rows[1]), :],
            q_got.at[0].at[pl.ds(piece_rows[0], piece_rows[1]), :],
            slot_c,
            k,
            source,
            start=False,
        ).wait_recv()
    incoming = q_got[0]
    is_head = group == 0
    identity = jnp.concatenate(
        [jnp.zeros((quarter, half), jnp.float32), jnp.ones((8, half), jnp.float32)], axis=0
    )
    q_state[0] = jnp.where(is_head, identity, incoming)
    landing = 1
    for level, (spread_width, ks) in enumerate(levels):
        arrivals = []
        for k in ks:
            arrivals.append((k, copy(q_state.at[level], q_got.at[landing], 4 + level, k - 1, order + 8 * k * spread_width), landing))
            landing += 1
        held = q_state[level]
        for k, handle, spot in arrivals:
            handle.wait_recv()
            came = q_got[spot]
            scale = held[quarter : quarter + 1, :]
            combined = jnp.concatenate([held[:quarter] + scale * came[:quarter], held[quarter:] * came[quarter:]], axis=0)
            held = jnp.where(group >= k * spread_width, combined, held)
        q_state[level + 1] = held
    depth = len(levels)
    prefix = q_state.at[depth].at[pl.ds(0, quarter), :]
    spread_copies = [copy(prefix, gathered.at[t - 1], slot_e, t - 1, order - index + (index + t) % 8) for t in range(1, 8)]
    for handle in sides + spread_copies:
        handle.wait_recv()
    at_start = ring == 0
    for t in range(8):
        owner = (index - t + 8) % 8
        owner_ring, owner_core = (owner // 2, owner % 2)
        band = pl.ds(pl.multiple_of(owner_ring * quarter, quarter), quarter)
        piece = q_state[depth, :quarter, :] if t == 0 else gathered[t - 1]
        left_side = owner_core == 0
        low = jnp.where(first, final[1, band, :], final[2, band, :])
        low_scale = jnp.where(first, final[1, factor_row, :], final[2, factor_row, :])
        high = jnp.where(first, final[0, band, :], final[1, band, :])
        high_scale = jnp.where(first, final[0, factor_row, :], final[1, factor_row, :])
        before = jnp.where(left_side, low, high)
        before_scale = jnp.where(left_side, low_scale, high_scale)
        behind = jnp.where(at_start, piece, before + before_scale * piece)
        element = jnp.where(left_side, pair[band, :], got[0, band, :])
        element_scale = jnp.where(left_side, pair[factor_row, :], got[0, factor_row, :])
        cols = pl.ds(pl.multiple_of(owner_core * half, half), half)
        out_ref[band, cols] = jnp.where(first, behind, element + element_scale * behind)
    if carry:
        carry_out[...] = held_carry[...]
    for handle in started:
        handle.wait_send()

    @pl.when(last_of_ring)
    def _():
        scatter(False)


def kernel_scan(factor, offset, reverse, ident, carried=None):
    size = lax.axis_size("depth")
    rows, width = offset.shape
    half = width // 2
    spread = jnp.broadcast_to(factor[None, :], (8, width))
    packed = jnp.concatenate([offset, spread], axis=0)
    groups = size // 8
    links = sum(step - 1 for step in radices(groups))
    levels = len(radices(groups))
    quarter = rows // 4
    carry = carried is not None
    result = jax.ShapeDtypeStruct((rows, width), jnp.float32)
    place = pl.BlockSpec(memory_space=pltpu.VMEM)
    extra = [pltpu.VMEM((rows, width), jnp.float32)] if carry else []
    return pl.pallas_call(
        functools.partial(group_kernel, size, reverse, 4, carry),
        out_shape=(result, result) if carry else result,
        in_specs=[place, place] if carry else [place],
        out_specs=(place, place) if carry else place,
        scratch_shapes=[
            pltpu.VMEM((3, rows + 8, half), jnp.float32),
            pltpu.VMEM((3, rows + 8, half), jnp.float32),
            pltpu.VMEM((links + 1, quarter + 8, half), jnp.float32),
            pltpu.VMEM((levels + 1, quarter + 8, half), jnp.float32),
            pltpu.VMEM((7, quarter, half), jnp.float32),
            pltpu.VMEM((3, rows + 8, half), jnp.float32),
            pltpu.VMEM((rows + 8, half), jnp.float32),
        ]
        + extra
        + [
            pltpu.SemaphoreType.DMA((6 + levels, 8)),
            pltpu.SemaphoreType.DMA((6 + levels, 8)),
        ],
        compiler_params=pltpu.CompilerParams(collective_id=ident, has_side_effects=True),
    )(*((packed, carried) if carry else (packed,)))


def prepare_block(state, w_first, gain_row):
    inverse = lax.rsqrt(jnp.mean(state * state, axis=-1, keepdims=True) + 1e-05)
    normed = (state * inverse * gain_row).astype(jnp.bfloat16)
    preact = jnp.dot(normed, w_first, preferred_element_type=jnp.float32)
    return (inverse, preact)


def finish_block(state, preact, w_second, decay_row):
    hidden = jax.nn.silu(preact).astype(jnp.bfloat16)
    return decay_row * state + jnp.dot(hidden, w_second, preferred_element_type=jnp.float32)


def backward_block(state, inverse, preact, upstream, w_first, w_second, gain_row, decay_row):
    grad_hidden = lax.dot_general(
        upstream.astype(jnp.bfloat16),
        w_second,
        (((1,), (1,)), ((), ())),
        preferred_element_type=jnp.float32,
    )
    sigma = jax.nn.sigmoid(preact)
    grad_pre = (grad_hidden * sigma * (1.0 + preact * (1.0 - sigma))).astype(jnp.bfloat16)
    grad_norm = lax.dot_general(
        grad_pre, w_first, (((1,), (1,)), ((), ())), preferred_element_type=jnp.float32
    )
    scaled = grad_norm * gain_row
    inner = jnp.mean(scaled * state, axis=-1, keepdims=True)
    return decay_row * upstream + inverse * scaled - state * inverse**3 * inner


def relax_forward(start, w_in, w_out, norm_gain, decay, want_end):
    state = start
    count = w_in.shape[0]
    states_list, inverse_list, preact_list = ([], [], [])
    for block in range(count):
        states_list.append(state)
        inverse, preact = prepare_block(state, w_in[block], norm_gain[block])
        inverse_list.append(inverse)
        preact_list.append(preact)
        if want_end or block + 1 < count:
            state = finish_block(state, preact, w_out[block], decay[block])
    return (state, states_list, inverse_list, preact_list)


def relax_backward(start, states, inverses, preacts, w_in, w_out, norm_gain, decay):
    adjoint = start
    count = w_in.shape[0]
    collected = [None] * count
    for block in reversed(range(count)):
        adjoint = backward_block(
            states[block],
            inverses[block],
            preacts[block],
            adjoint,
            w_in[block],
            w_out[block],
            norm_gain[block],
            decay[block],
        )
        collected[block] = adjoint
    return (adjoint, collected)


def compose(earlier, later):
    return (later[0] * earlier[0], later[0] * earlier[1] + later[1])


def shards(state_guess, adjoint_guess, w_in, w_out, norm_gain, decay):
    factor = jnp.prod(decay, axis=0)
    guess_state = state_guess[0]
    guess_adjoint = adjoint_guess[0]
    next_guess = shifted(guess_state, "depth", -1)
    end_state, _, _, _ = relax_forward(guess_state, w_in, w_out, norm_gain, decay, True)
    correction, prev_guess = kernel_scan(factor, end_state - next_guess, False, 0, guess_adjoint)
    start = guess_state + correction
    _, states, inverses, preacts = relax_forward(start, w_in, w_out, norm_gain, decay, False)
    first_adjoint, _ = relax_backward(
        guess_adjoint, states, inverses, preacts, w_in, w_out, norm_gain, decay
    )
    eps = kernel_scan(factor, first_adjoint - prev_guess, True, 1)
    head = guess_adjoint + eps
    _, lambdas = relax_backward(head, states, inverses, preacts, w_in, w_out, norm_gain, decay)
    return (jnp.stack(states), jnp.stack(lambdas))


def solution(mesh):
    placed = (
        P("depth", None, None),
        P("depth", None, None),
        P("depth", None, None),
        P("depth", None, None),
        P("depth", None),
        P("depth", None),
    )
    return jax.shard_map(
        shards,
        mesh=mesh,
        in_specs=placed,
        out_specs=(P("depth", None, None), P("depth", None, None)),
        check_vma=False,
    )
```

```python
import functools

import jax
import jax.numpy as jnp
from jax import lax
from jax.experimental import pallas as pl
from jax.experimental.pallas import tpu as pltpu
from jax.sharding import PartitionSpec as P


def shifted(block, axis, distance):
    devices = range(lax.axis_size(axis))
    route = [(i - distance, i) for i in devices if i - distance in devices]
    return lax.ppermute(block, axis, route)


MESH = pl.DeviceIdType.MESH


def radices(groups):
    along_z = min(groups, 8)
    out = []
    for part in (along_z, groups // along_z):
        while part > 1:
            step = 4 if part % 4 == 0 else 2
            out.append(step)
            part //= step
    return out


def group_kernel(size, reverse, pieces, packed_ref, out_ref, got, state, q_got, q_state, gathered, final, pair, sends, recvs):
    position = lax.axis_index("depth")
    order = size - 1 - position if reverse else position
    core, chip = (order % 2, order // 2)
    ring, group = (chip % 4, chip // 4)
    rows = out_ref.shape[0]
    half = packed_ref.shape[1] // 2
    groups = size // 8
    quarter = rows // 4
    step_rows = rows // pieces
    spans = [(rows, 8)] + [(k * step_rows, step_rows) for k in range(pieces)]
    levels = []
    width_now = 1
    for step in radices(groups):
        levels.append((width_now, list(range(1, step))))
        width_now *= step
    links = [(level, k) for level, (_, ks) in enumerate(levels) for k in ks]
    slot_c, slot_e, slot_f = (3, 4 + len(levels), 5 + len(levels))
    index = order % 8

    def device(q):
        q = lax.rem(q + 2 * size, size)
        return (size - 1 - q if reverse else q,)

    def in_ring(step):
        return order + 2 * ((ring + step + 4) % 4 - ring)

    partner = order + 1 - 2 * core
    source = order - 8 + 2 * (3 - ring)
    sinks = [order + 8 + 2 * (k - 3) for k in range(4)]
    targets = [order + 8 + 2 * (k - ring) for k in range(4)]
    targets += [order - 8 + 2 * (k - ring) for k in range(4)]
    for spread_width, ks in levels:
        targets += [order + 8 * k * spread_width for k in ks] + [order - 8 * k * spread_width for k in ks]
    targets += [order - index + (index + t) % 8 for t in range(1, 8)]
    targets += [order + 1, order - 1, order + 2, order - 2, order + 3, order - 3]
    barrier = pltpu.get_barrier_semaphore()
    for target in targets:
        pl.semaphore_signal(barrier, inc=1, device_id=device(target), device_id_type=MESH)
    last_of_ring = ring == 3
    pl.semaphore_wait(barrier, len(targets))

    started = []

    def copy(src, dst, slot, piece, target, start=True, keep=True, landing=None):
        handle = pltpu.make_async_remote_copy(
            src_ref=src,
            dst_ref=dst,
            send_sem=sends.at[slot, piece],
            recv_sem=recvs.at[slot, piece if landing is None else landing],
            device_id=device(target),
            device_id_type=MESH,
        )
        if start:
            handle.start()
        if start and keep:
            started.append(handle)
        return handle

    def block(ref, piece):
        first_row, count = spans[piece]
        return ref.at[pl.ds(first_row, count), :]

    first = core == 0
    factor_row = slice(rows, rows + 1)
    mine_ref = packed_ref.at[:, pl.ds(pl.multiple_of(core * half, half), half)]
    other_ref = packed_ref.at[:, pl.ds(pl.multiple_of((1 - core) * half, half), half)]
    pending = [copy(block(other_ref, k), block(got.at[0], k), 0, k, partner) for k in range(pieces + 1)]
    for stage in range(3):
        following = []
        for piece in range(pieces + 1):
            first_row, count = spans[piece]
            part = slice(first_row, first_row + count)
            pending[piece].wait_recv()
            came = got[stage, part, :]
            if stage == 0:
                mine = mine_ref[part, :]
                later = jnp.where(first, came, mine)
                earlier = jnp.where(first, mine, came)
                scale = jnp.where(first, got[0, factor_row, :], mine_ref[factor_row, :])
                value = later * earlier if piece == 0 else later + scale * earlier
            else:
                held = state[stage - 1, part, :]
                scale = state[stage - 1, factor_row, :]
                combined = held * came if piece == 0 else held + scale * came
                value = jnp.where(ring >= stage, combined, held)
            state[stage, part, :] = value
            if stage < 2:
                step = 1 if stage == 0 else 2
                following.append(
                    copy(block(state.at[stage], piece), block(got.at[stage + 1], piece), stage + 1, piece, in_ring(step))
                )
        pending = following

    sides = [copy(state.at[2], final.at[k], slot_f, k, order + 1 + k) for k in range(3)]
    sides.append(copy(mine_ref, pair, slot_f, 3, partner))

    def scatter(start):
        for k in range(4):
            for piece, (first_row, count, landing) in enumerate(((k * quarter, quarter, 0), (rows, 8, quarter))):
                handle = copy(
                    state.at[2].at[pl.ds(first_row, count), :],
                    q_got.at[0].at[pl.ds(landing, count), :],
                    slot_c,
                    2 * k + piece,
                    sinks[k],
                    start=start,
                    keep=False,
                    landing=piece,
                )
                if not start:
                    handle.wait_send()

    @pl.when(last_of_ring)
    def _():
        scatter(True)

    for k, piece_rows in ((0, (0, quarter)), (1, (quarter, 8))):
        copy(
            state.at[2].at[pl.ds(piece_rows[0], piece_rows[1]), :],
            q_got.at[0].at[pl.ds(piece_rows[0], piece_rows[1]), :],
            slot_c,
            k,
            source,
            start=False,
        ).wait_recv()
    incoming = q_got[0]
    is_head = group == 0
    identity = jnp.concatenate(
        [jnp.zeros((quarter, half), jnp.float32), jnp.ones((8, half), jnp.float32)], axis=0
    )
    q_state[0] = jnp.where(is_head, identity, incoming)
    landing = 1
    for level, (spread_width, ks) in enumerate(levels):
        arrivals = []
        for k in ks:
            arrivals.append((k, copy(q_state.at[level], q_got.at[landing], 4 + level, k - 1, order + 8 * k * spread_width), landing))
            landing += 1
        held = q_state[level]
        for k, handle, spot in arrivals:
            handle.wait_recv()
            came = q_got[spot]
            scale = held[quarter : quarter + 1, :]
            combined = jnp.concatenate([held[:quarter] + scale * came[:quarter], held[quarter:] * came[quarter:]], axis=0)
            held = jnp.where(group >= k * spread_width, combined, held)
        q_state[level + 1] = held
    depth = len(levels)
    prefix = q_state.at[depth].at[pl.ds(0, quarter), :]
    spread_copies = [copy(prefix, gathered.at[t - 1], slot_e, t - 1, order - index + (index + t) % 8) for t in range(1, 8)]
    for handle in sides + spread_copies:
        handle.wait_recv()
    at_start = ring == 0
    for t in range(8):
        owner = (index - t + 8) % 8
        owner_ring, owner_core = (owner // 2, owner % 2)
        band = pl.ds(pl.multiple_of(owner_ring * quarter, quarter), quarter)
        piece = q_state[depth, :quarter, :] if t == 0 else gathered[t - 1]
        left_side = owner_core == 0
        low = jnp.where(first, final[1, band, :], final[2, band, :])
        low_scale = jnp.where(first, final[1, factor_row, :], final[2, factor_row, :])
        high = jnp.where(first, final[0, band, :], final[1, band, :])
        high_scale = jnp.where(first, final[0, factor_row, :], final[1, factor_row, :])
        before = jnp.where(left_side, low, high)
        before_scale = jnp.where(left_side, low_scale, high_scale)
        behind = jnp.where(at_start, piece, before + before_scale * piece)
        element = jnp.where(left_side, pair[band, :], got[0, band, :])
        element_scale = jnp.where(left_side, pair[factor_row, :], got[0, factor_row, :])
        cols = pl.ds(pl.multiple_of(owner_core * half, half), half)
        out_ref[band, cols] = jnp.where(first, behind, element + element_scale * behind)
    for handle in started:
        handle.wait_send()

    @pl.when(last_of_ring)
    def _():
        scatter(False)


def kernel_scan(factor, offset, reverse, ident):
    size = lax.axis_size("depth")
    rows, width = offset.shape
    half = width // 2
    spread = jnp.broadcast_to(factor[None, :], (8, width))
    packed = jnp.concatenate([offset, spread], axis=0)
    groups = size // 8
    links = sum(step - 1 for step in radices(groups))
    levels = len(radices(groups))
    quarter = rows // 4
    return pl.pallas_call(
        functools.partial(group_kernel, size, reverse, 2),
        out_shape=jax.ShapeDtypeStruct((rows, width), jnp.float32),
        in_specs=[pl.BlockSpec(memory_space=pltpu.VMEM)],
        out_specs=pl.BlockSpec(memory_space=pltpu.VMEM),
        scratch_shapes=[
            pltpu.VMEM((3, rows + 8, half), jnp.float32),
            pltpu.VMEM((3, rows + 8, half), jnp.float32),
            pltpu.VMEM((links + 1, quarter + 8, half), jnp.float32),
            pltpu.VMEM((levels + 1, quarter + 8, half), jnp.float32),
            pltpu.VMEM((7, quarter, half), jnp.float32),
            pltpu.VMEM((3, rows + 8, half), jnp.float32),
            pltpu.VMEM((rows + 8, half), jnp.float32),
            pltpu.SemaphoreType.DMA((6 + levels, 8)),
            pltpu.SemaphoreType.DMA((6 + levels, 8)),
        ],
        compiler_params=pltpu.CompilerParams(collective_id=ident, has_side_effects=True),
    )(packed)


def prepare_block(state, w_first, gain_row):
    inverse = lax.rsqrt(jnp.mean(state * state, axis=-1, keepdims=True) + 1e-05)
    normed = (state * inverse * gain_row).astype(jnp.bfloat16)
    preact = jnp.dot(normed, w_first, preferred_element_type=jnp.float32)
    return (inverse, preact)


def finish_block(state, preact, w_second, decay_row):
    hidden = jax.nn.silu(preact).astype(jnp.bfloat16)
    return decay_row * state + jnp.dot(hidden, w_second, preferred_element_type=jnp.float32)


def backward_block(state, inverse, preact, upstream, w_first, w_second, gain_row, decay_row):
    grad_hidden = lax.dot_general(
        upstream.astype(jnp.bfloat16),
        w_second,
        (((1,), (1,)), ((), ())),
        preferred_element_type=jnp.float32,
    )
    sigma = jax.nn.sigmoid(preact)
    grad_pre = (grad_hidden * sigma * (1.0 + preact * (1.0 - sigma))).astype(jnp.bfloat16)
    grad_norm = lax.dot_general(
        grad_pre, w_first, (((1,), (1,)), ((), ())), preferred_element_type=jnp.float32
    )
    scaled = grad_norm * gain_row
    inner = jnp.mean(scaled * state, axis=-1, keepdims=True)
    return decay_row * upstream + inverse * scaled - state * inverse**3 * inner


def relax_forward(start, w_in, w_out, norm_gain, decay, want_end):
    state = start
    count = w_in.shape[0]
    states_list, inverse_list, preact_list = ([], [], [])
    for block in range(count):
        states_list.append(state)
        inverse, preact = prepare_block(state, w_in[block], norm_gain[block])
        inverse_list.append(inverse)
        preact_list.append(preact)
        if want_end or block + 1 < count:
            state = finish_block(state, preact, w_out[block], decay[block])
    return (state, states_list, inverse_list, preact_list)


def relax_backward(start, states, inverses, preacts, w_in, w_out, norm_gain, decay):
    adjoint = start
    count = w_in.shape[0]
    collected = [None] * count
    for block in reversed(range(count)):
        adjoint = backward_block(
            states[block],
            inverses[block],
            preacts[block],
            adjoint,
            w_in[block],
            w_out[block],
            norm_gain[block],
            decay[block],
        )
        collected[block] = adjoint
    return (adjoint, collected)


def compose(earlier, later):
    return (later[0] * earlier[0], later[0] * earlier[1] + later[1])


def shards(state_guess, adjoint_guess, w_in, w_out, norm_gain, decay):
    factor = jnp.prod(decay, axis=0)
    guess_state = state_guess[0]
    guess_adjoint = adjoint_guess[0]
    next_guess = shifted(guess_state, "depth", -1)
    prev_guess = shifted(guess_adjoint, "depth", 1)
    end_state, _, _, _ = relax_forward(guess_state, w_in, w_out, norm_gain, decay, True)
    correction = kernel_scan(factor, end_state - next_guess, False, 0)
    start = guess_state + correction
    _, states, inverses, preacts = relax_forward(start, w_in, w_out, norm_gain, decay, False)
    first_adjoint, _ = relax_backward(
        guess_adjoint, states, inverses, preacts, w_in, w_out, norm_gain, decay
    )
    eps = kernel_scan(factor, first_adjoint - prev_guess, True, 1)
    head = guess_adjoint + eps
    _, lambdas = relax_backward(head, states, inverses, preacts, w_in, w_out, norm_gain, decay)
    return (jnp.stack(states), jnp.stack(lambdas))


def solution(mesh):
    placed = (
        P("depth", None, None),
        P("depth", None, None),
        P("depth", None, None),
        P("depth", None, None),
        P("depth", None),
        P("depth", None),
    )
    return jax.shard_map(
        shards,
        mesh=mesh,
        in_specs=placed,
        out_specs=(P("depth", None, None), P("depth", None, None)),
        check_vma=False,
    )
```

```python
import functools

import jax
import jax.numpy as jnp
from jax import lax
from jax.experimental import pallas as pl
from jax.experimental.pallas import tpu as pltpu
from jax.sharding import PartitionSpec as P


def shifted(block, axis, distance):
    devices = range(lax.axis_size(axis))
    route = [(i - distance, i) for i in devices if i - distance in devices]
    return lax.ppermute(block, axis, route)


MESH = pl.DeviceIdType.MESH


def radices(groups):
    along_z = min(groups, 8)
    out = []
    for part in (along_z, groups // along_z):
        while part > 1:
            step = 4 if part % 4 == 0 else 2
            out.append(step)
            part //= step
    return out


def group_kernel(size, reverse, pieces, packed_ref, out_ref, got, state, q_got, q_state, gathered, final, pair, sends, recvs):
    position = lax.axis_index("depth")
    order = size - 1 - position if reverse else position
    core, chip = (order % 2, order // 2)
    ring, group = (chip % 4, chip // 4)
    rows = out_ref.shape[0]
    half = packed_ref.shape[1] // 2
    groups = size // 8
    quarter = rows // 4
    step_rows = rows // pieces
    spans = [(rows, 8)] + [(k * step_rows, step_rows) for k in range(pieces)]
    levels = []
    width_now = 1
    for step in radices(groups):
        levels.append((width_now, list(range(1, step))))
        width_now *= step
    links = [(level, k) for level, (_, ks) in enumerate(levels) for k in ks]
    slot_c, slot_e, slot_f = (3, 4 + len(levels), 5 + len(levels))
    index = order % 8

    def device(q):
        q = lax.rem(q + 2 * size, size)
        return (size - 1 - q if reverse else q,)

    def in_ring(step):
        return order + 2 * ((ring + step + 4) % 4 - ring)

    partner = order + 1 - 2 * core
    source = order - 8 + 2 * (3 - ring)
    sinks = [order + 8 + 2 * (k - 3) for k in range(4)]
    targets = [order + 8 + 2 * (k - ring) for k in range(4)]
    targets += [order - 8 + 2 * (k - ring) for k in range(4)]
    for spread_width, ks in levels:
        targets += [order + 8 * k * spread_width for k in ks] + [order - 8 * k * spread_width for k in ks]
    targets += [order - index + (index + t) % 8 for t in range(1, 8)]
    targets += [order + 1, order - 1, order + 2, order - 2, order + 3, order - 3]
    barrier = pltpu.get_barrier_semaphore()
    for target in targets:
        pl.semaphore_signal(barrier, inc=1, device_id=device(target), device_id_type=MESH)
    last_of_ring = ring == 3
    pl.semaphore_wait(barrier, len(targets))

    started = []

    def copy(src, dst, slot, piece, target, start=True, keep=True, landing=None):
        handle = pltpu.make_async_remote_copy(
            src_ref=src,
            dst_ref=dst,
            send_sem=sends.at[slot, piece],
            recv_sem=recvs.at[slot, piece if landing is None else landing],
            device_id=device(target),
            device_id_type=MESH,
        )
        if start:
            handle.start()
        if start and keep:
            started.append(handle)
        return handle

    def block(ref, piece):
        first_row, count = spans[piece]
        return ref.at[pl.ds(first_row, count), :]

    first = core == 0
    factor_row = slice(rows, rows + 1)
    mine_ref = packed_ref.at[:, pl.ds(pl.multiple_of(core * half, half), half)]
    other_ref = packed_ref.at[:, pl.ds(pl.multiple_of((1 - core) * half, half), half)]
    pending = [copy(block(other_ref, k), block(got.at[0], k), 0, k, partner) for k in range(pieces + 1)]
    for stage in range(3):
        following = []
        for piece in range(pieces + 1):
            first_row, count = spans[piece]
            part = slice(first_row, first_row + count)
            pending[piece].wait_recv()
            came = got[stage, part, :]
            if stage == 0:
                mine = mine_ref[part, :]
                later = jnp.where(first, came, mine)
                earlier = jnp.where(first, mine, came)
                scale = jnp.where(first, got[0, factor_row, :], mine_ref[factor_row, :])
                value = later * earlier if piece == 0 else later + scale * earlier
            else:
                held = state[stage - 1, part, :]
                scale = state[stage - 1, factor_row, :]
                combined = held * came if piece == 0 else held + scale * came
                value = jnp.where(ring >= stage, combined, held)
            state[stage, part, :] = value
            if stage < 2:
                step = 1 if stage == 0 else 2
                following.append(
                    copy(block(state.at[stage], piece), block(got.at[stage + 1], piece), stage + 1, piece, in_ring(step))
                )
        pending = following

    sides = [copy(state.at[2], final.at[k], slot_f, k, order + 1 + k) for k in range(3)]
    sides.append(copy(mine_ref, pair, slot_f, 3, partner))

    def scatter(start):
        for k in range(4):
            for piece, (first_row, count, landing) in enumerate(((k * quarter, quarter, 0), (rows, 8, quarter))):
                handle = copy(
                    state.at[2].at[pl.ds(first_row, count), :],
                    q_got.at[0].at[pl.ds(landing, count), :],
                    slot_c,
                    2 * k + piece,
                    sinks[k],
                    start=start,
                    keep=False,
                    landing=piece,
                )
                if not start:
                    handle.wait_send()

    @pl.when(last_of_ring)
    def _():
        scatter(True)

    for k, piece_rows in ((0, (0, quarter)), (1, (quarter, 8))):
        copy(
            state.at[2].at[pl.ds(piece_rows[0], piece_rows[1]), :],
            q_got.at[0].at[pl.ds(piece_rows[0], piece_rows[1]), :],
            slot_c,
            k,
            source,
            start=False,
        ).wait_recv()
    incoming = q_got[0]
    is_head = group == 0
    identity = jnp.concatenate(
        [jnp.zeros((quarter, half), jnp.float32), jnp.ones((8, half), jnp.float32)], axis=0
    )
    q_state[0] = jnp.where(is_head, identity, incoming)
    landing = 1
    for level, (spread_width, ks) in enumerate(levels):
        arrivals = []
        for k in ks:
            arrivals.append((k, copy(q_state.at[level], q_got.at[landing], 4 + level, k - 1, order + 8 * k * spread_width), landing))
            landing += 1
        held = q_state[level]
        for k, handle, spot in arrivals:
            handle.wait_recv()
            came = q_got[spot]
            scale = held[quarter : quarter + 1, :]
            combined = jnp.concatenate([held[:quarter] + scale * came[:quarter], held[quarter:] * came[quarter:]], axis=0)
            held = jnp.where(group >= k * spread_width, combined, held)
        q_state[level + 1] = held
    depth = len(levels)
    prefix = q_state.at[depth].at[pl.ds(0, quarter), :]
    spread_copies = [copy(prefix, gathered.at[t - 1], slot_e, t - 1, order - index + (index + t) % 8) for t in range(1, 8)]
    for handle in sides + spread_copies:
        handle.wait_recv()
    at_start = ring == 0

    def finish(side):
        low, high = ((final.at[1], final.at[0]) if side == 0 else (final.at[2], final.at[1]))
        for t in range(8):
            owner = (index - t + 8) % 8
            owner_core = (side - t) % 2
            band = pl.ds(pl.multiple_of((owner // 2) * quarter, quarter), quarter)
            piece = q_state[depth, :quarter, :] if t == 0 else gathered[t - 1]
            before = low if owner_core == 0 else high
            behind = jnp.where(at_start, piece, before[band, :] + before[factor_row, :] * piece)
            cols = slice(owner_core * half, (owner_core + 1) * half)
            if side == 0:
                out_ref[band, cols] = behind
            else:
                element = pair if owner_core == 0 else got.at[0]
                out_ref[band, cols] = element[band, :] + element[factor_row, :] * behind

    @pl.when(first)
    def _():
        finish(0)

    @pl.when(jnp.logical_not(first))
    def _():
        finish(1)

    for handle in started:
        handle.wait_send()

    @pl.when(last_of_ring)
    def _():
        scatter(False)


def kernel_scan(factor, offset, reverse, ident):
    size = lax.axis_size("depth")
    rows, width = offset.shape
    half = width // 2
    spread = jnp.broadcast_to(factor[None, :], (8, width))
    packed = jnp.concatenate([offset, spread], axis=0)
    groups = size // 8
    links = sum(step - 1 for step in radices(groups))
    levels = len(radices(groups))
    quarter = rows // 4
    return pl.pallas_call(
        functools.partial(group_kernel, size, reverse, 4),
        out_shape=jax.ShapeDtypeStruct((rows, width), jnp.float32),
        in_specs=[pl.BlockSpec(memory_space=pltpu.VMEM)],
        out_specs=pl.BlockSpec(memory_space=pltpu.VMEM),
        scratch_shapes=[
            pltpu.VMEM((3, rows + 8, half), jnp.float32),
            pltpu.VMEM((3, rows + 8, half), jnp.float32),
            pltpu.VMEM((links + 1, quarter + 8, half), jnp.float32),
            pltpu.VMEM((levels + 1, quarter + 8, half), jnp.float32),
            pltpu.VMEM((7, quarter, half), jnp.float32),
            pltpu.VMEM((3, rows + 8, half), jnp.float32),
            pltpu.VMEM((rows + 8, half), jnp.float32),
            pltpu.SemaphoreType.DMA((6 + levels, 8)),
            pltpu.SemaphoreType.DMA((6 + levels, 8)),
        ],
        compiler_params=pltpu.CompilerParams(collective_id=ident, has_side_effects=True),
    )(packed)


def prepare_block(state, w_first, gain_row):
    inverse = lax.rsqrt(jnp.mean(state * state, axis=-1, keepdims=True) + 1e-05)
    normed = (state * inverse * gain_row).astype(jnp.bfloat16)
    preact = jnp.dot(normed, w_first, preferred_element_type=jnp.float32)
    return (inverse, preact)


def finish_block(state, preact, w_second, decay_row):
    hidden = jax.nn.silu(preact).astype(jnp.bfloat16)
    return decay_row * state + jnp.dot(hidden, w_second, preferred_element_type=jnp.float32)


def backward_block(state, inverse, preact, upstream, w_first, w_second, gain_row, decay_row):
    grad_hidden = lax.dot_general(
        upstream.astype(jnp.bfloat16),
        w_second,
        (((1,), (1,)), ((), ())),
        preferred_element_type=jnp.float32,
    )
    sigma = jax.nn.sigmoid(preact)
    grad_pre = (grad_hidden * sigma * (1.0 + preact * (1.0 - sigma))).astype(jnp.bfloat16)
    grad_norm = lax.dot_general(
        grad_pre, w_first, (((1,), (1,)), ((), ())), preferred_element_type=jnp.float32
    )
    scaled = grad_norm * gain_row
    inner = jnp.mean(scaled * state, axis=-1, keepdims=True)
    return decay_row * upstream + inverse * scaled - state * inverse**3 * inner


def relax_forward(start, w_in, w_out, norm_gain, decay, want_end):
    state = start
    count = w_in.shape[0]
    states_list, inverse_list, preact_list = ([], [], [])
    for block in range(count):
        states_list.append(state)
        inverse, preact = prepare_block(state, w_in[block], norm_gain[block])
        inverse_list.append(inverse)
        preact_list.append(preact)
        if want_end or block + 1 < count:
            state = finish_block(state, preact, w_out[block], decay[block])
    return (state, states_list, inverse_list, preact_list)


def relax_backward(start, states, inverses, preacts, w_in, w_out, norm_gain, decay):
    adjoint = start
    count = w_in.shape[0]
    collected = [None] * count
    for block in reversed(range(count)):
        adjoint = backward_block(
            states[block],
            inverses[block],
            preacts[block],
            adjoint,
            w_in[block],
            w_out[block],
            norm_gain[block],
            decay[block],
        )
        collected[block] = adjoint
    return (adjoint, collected)


def compose(earlier, later):
    return (later[0] * earlier[0], later[0] * earlier[1] + later[1])


def shards(state_guess, adjoint_guess, w_in, w_out, norm_gain, decay):
    factor = jnp.prod(decay, axis=0)
    guess_state = state_guess[0]
    guess_adjoint = adjoint_guess[0]
    next_guess = shifted(guess_state, "depth", -1)
    prev_guess = shifted(guess_adjoint, "depth", 1)
    end_state, _, _, _ = relax_forward(guess_state, w_in, w_out, norm_gain, decay, True)
    correction = kernel_scan(factor, end_state - next_guess, False, 0)
    start = guess_state + correction
    _, states, inverses, preacts = relax_forward(start, w_in, w_out, norm_gain, decay, False)
    first_adjoint, _ = relax_backward(
        guess_adjoint, states, inverses, preacts, w_in, w_out, norm_gain, decay
    )
    eps = kernel_scan(factor, first_adjoint - prev_guess, True, 1)
    head = guess_adjoint + eps
    _, lambdas = relax_backward(head, states, inverses, preacts, w_in, w_out, norm_gain, decay)
    return (jnp.stack(states), jnp.stack(lambdas))


def solution(mesh):
    placed = (
        P("depth", None, None),
        P("depth", None, None),
        P("depth", None, None),
        P("depth", None, None),
        P("depth", None),
        P("depth", None),
    )
    return jax.shard_map(
        shards,
        mesh=mesh,
        in_specs=placed,
        out_specs=(P("depth", None, None), P("depth", None, None)),
        check_vma=False,
    )
```

```python
import functools

import jax
import jax.numpy as jnp
from jax import lax
from jax.experimental import pallas as pl
from jax.experimental.pallas import tpu as pltpu
from jax.sharding import PartitionSpec as P


def shifted(block, axis, distance):
    devices = range(lax.axis_size(axis))
    route = [(i - distance, i) for i in devices if i - distance in devices]
    return lax.ppermute(block, axis, route)


MESH = pl.DeviceIdType.MESH


def radices(groups):
    along_z = min(groups, 8)
    out = []
    for part in (along_z, groups // along_z):
        while part > 1:
            step = 2 if part % 8 == 0 else (4 if part % 4 == 0 else 2)
            out.append(step)
            part //= step
    return out


def group_kernel(size, reverse, pieces, packed_ref, out_ref, got, state, q_got, q_state, gathered, final, pair, sends, recvs):
    position = lax.axis_index("depth")
    order = size - 1 - position if reverse else position
    core, chip = (order % 2, order // 2)
    ring, group = (chip % 4, chip // 4)
    rows = out_ref.shape[0]
    half = packed_ref.shape[1] // 2
    groups = size // 8
    quarter = rows // 4
    step_rows = rows // pieces
    spans = [(rows, 8)] + [(k * step_rows, step_rows) for k in range(pieces)]
    levels = []
    width_now = 1
    for step in radices(groups):
        levels.append((width_now, list(range(1, step))))
        width_now *= step
    links = [(level, k) for level, (_, ks) in enumerate(levels) for k in ks]
    slot_c, slot_e, slot_f = (3, 4 + len(levels), 5 + len(levels))
    index = order % 8

    def device(q):
        q = lax.rem(q + 2 * size, size)
        return (size - 1 - q if reverse else q,)

    def in_ring(step):
        return order + 2 * ((ring + step + 4) % 4 - ring)

    partner = order + 1 - 2 * core
    source = order - 8 + 2 * (3 - ring)
    sinks = [order + 8 + 2 * (k - 3) for k in range(4)]
    targets = [order + 8 + 2 * (k - ring) for k in range(4)]
    targets += [order - 8 + 2 * (k - ring) for k in range(4)]
    for spread_width, ks in levels:
        targets += [order + 8 * k * spread_width for k in ks] + [order - 8 * k * spread_width for k in ks]
    targets += [order - index + (index + t) % 8 for t in range(1, 8)]
    targets += [order + 1, order - 1, order + 2, order - 2, order + 3, order - 3]
    barrier = pltpu.get_barrier_semaphore()
    for target in targets:
        pl.semaphore_signal(barrier, inc=1, device_id=device(target), device_id_type=MESH)
    last_of_ring = ring == 3
    pl.semaphore_wait(barrier, len(targets))

    started = []

    def copy(src, dst, slot, piece, target, start=True, keep=True, landing=None):
        handle = pltpu.make_async_remote_copy(
            src_ref=src,
            dst_ref=dst,
            send_sem=sends.at[slot, piece],
            recv_sem=recvs.at[slot, piece if landing is None else landing],
            device_id=device(target),
            device_id_type=MESH,
        )
        if start:
            handle.start()
        if start and keep:
            started.append(handle)
        return handle

    def block(ref, piece):
        first_row, count = spans[piece]
        return ref.at[pl.ds(first_row, count), :]

    first = core == 0
    factor_row = slice(rows, rows + 1)
    mine_ref = packed_ref.at[:, pl.ds(pl.multiple_of(core * half, half), half)]
    other_ref = packed_ref.at[:, pl.ds(pl.multiple_of((1 - core) * half, half), half)]
    pending = [copy(block(other_ref, k), block(got.at[0], k), 0, k, partner) for k in range(pieces + 1)]
    for stage in range(3):
        following = []
        for piece in range(pieces + 1):
            first_row, count = spans[piece]
            part = slice(first_row, first_row + count)
            pending[piece].wait_recv()
            came = got[stage, part, :]
            if stage == 0:
                mine = mine_ref[part, :]
                later = jnp.where(first, came, mine)
                earlier = jnp.where(first, mine, came)
                scale = jnp.where(first, got[0, factor_row, :], mine_ref[factor_row, :])
                value = later * earlier if piece == 0 else later + scale * earlier
            else:
                held = state[stage - 1, part, :]
                scale = state[stage - 1, factor_row, :]
                combined = held * came if piece == 0 else held + scale * came
                value = jnp.where(ring >= stage, combined, held)
            state[stage, part, :] = value
            if stage < 2:
                step = 1 if stage == 0 else 2
                following.append(
                    copy(block(state.at[stage], piece), block(got.at[stage + 1], piece), stage + 1, piece, in_ring(step))
                )
        pending = following

    sides = [copy(state.at[2], final.at[k], slot_f, k, order + 1 + k) for k in range(3)]
    sides.append(copy(mine_ref, pair, slot_f, 3, partner))

    def scatter(start):
        for k in range(4):
            for piece, (first_row, count, landing) in enumerate(((k * quarter, quarter, 0), (rows, 8, quarter))):
                handle = copy(
                    state.at[2].at[pl.ds(first_row, count), :],
                    q_got.at[0].at[pl.ds(landing, count), :],
                    slot_c,
                    2 * k + piece,
                    sinks[k],
                    start=start,
                    keep=False,
                    landing=piece,
                )
                if not start:
                    handle.wait_send()

    @pl.when(last_of_ring)
    def _():
        scatter(True)

    for k, piece_rows in ((0, (0, quarter)), (1, (quarter, 8))):
        copy(
            state.at[2].at[pl.ds(piece_rows[0], piece_rows[1]), :],
            q_got.at[0].at[pl.ds(piece_rows[0], piece_rows[1]), :],
            slot_c,
            k,
            source,
            start=False,
        ).wait_recv()
    incoming = q_got[0]
    is_head = group == 0
    identity = jnp.concatenate(
        [jnp.zeros((quarter, half), jnp.float32), jnp.ones((8, half), jnp.float32)], axis=0
    )
    q_state[0] = jnp.where(is_head, identity, incoming)
    landing = 1
    for level, (spread_width, ks) in enumerate(levels):
        arrivals = []
        for k in ks:
            arrivals.append((k, copy(q_state.at[level], q_got.at[landing], 4 + level, k - 1, order + 8 * k * spread_width), landing))
            landing += 1
        held = q_state[level]
        for k, handle, spot in arrivals:
            handle.wait_recv()
            came = q_got[spot]
            scale = held[quarter : quarter + 1, :]
            combined = jnp.concatenate([held[:quarter] + scale * came[:quarter], held[quarter:] * came[quarter:]], axis=0)
            held = jnp.where(group >= k * spread_width, combined, held)
        q_state[level + 1] = held
    depth = len(levels)
    prefix = q_state.at[depth].at[pl.ds(0, quarter), :]
    spread_copies = [copy(prefix, gathered.at[t - 1], slot_e, t - 1, order - index + (index + t) % 8) for t in range(1, 8)]
    for handle in sides + spread_copies:
        handle.wait_recv()
    at_start = ring == 0
    for t in range(8):
        owner = (index - t + 8) % 8
        owner_ring, owner_core = (owner // 2, owner % 2)
        band = pl.ds(pl.multiple_of(owner_ring * quarter, quarter), quarter)
        piece = q_state[depth, :quarter, :] if t == 0 else gathered[t - 1]
        left_side = owner_core == 0
        low = jnp.where(first, final[1, band, :], final[2, band, :])
        low_scale = jnp.where(first, final[1, factor_row, :], final[2, factor_row, :])
        high = jnp.where(first, final[0, band, :], final[1, band, :])
        high_scale = jnp.where(first, final[0, factor_row, :], final[1, factor_row, :])
        before = jnp.where(left_side, low, high)
        before_scale = jnp.where(left_side, low_scale, high_scale)
        behind = jnp.where(at_start, piece, before + before_scale * piece)
        element = jnp.where(left_side, pair[band, :], got[0, band, :])
        element_scale = jnp.where(left_side, pair[factor_row, :], got[0, factor_row, :])
        cols = pl.ds(pl.multiple_of(owner_core * half, half), half)
        out_ref[band, cols] = jnp.where(first, behind, element + element_scale * behind)
    for handle in started:
        handle.wait_send()

    @pl.when(last_of_ring)
    def _():
        scatter(False)


def kernel_scan(factor, offset, reverse, ident):
    size = lax.axis_size("depth")
    rows, width = offset.shape
    half = width // 2
    spread = jnp.broadcast_to(factor[None, :], (8, width))
    packed = jnp.concatenate([offset, spread], axis=0)
    groups = size // 8
    links = sum(step - 1 for step in radices(groups))
    levels = len(radices(groups))
    quarter = rows // 4
    return pl.pallas_call(
        functools.partial(group_kernel, size, reverse, 4),
        out_shape=jax.ShapeDtypeStruct((rows, width), jnp.float32),
        in_specs=[pl.BlockSpec(memory_space=pltpu.VMEM)],
        out_specs=pl.BlockSpec(memory_space=pltpu.VMEM),
        scratch_shapes=[
            pltpu.VMEM((3, rows + 8, half), jnp.float32),
            pltpu.VMEM((3, rows + 8, half), jnp.float32),
            pltpu.VMEM((links + 1, quarter + 8, half), jnp.float32),
            pltpu.VMEM((levels + 1, quarter + 8, half), jnp.float32),
            pltpu.VMEM((7, quarter, half), jnp.float32),
            pltpu.VMEM((3, rows + 8, half), jnp.float32),
            pltpu.VMEM((rows + 8, half), jnp.float32),
            pltpu.SemaphoreType.DMA((6 + levels, 8)),
            pltpu.SemaphoreType.DMA((6 + levels, 8)),
        ],
        compiler_params=pltpu.CompilerParams(collective_id=ident, has_side_effects=True),
    )(packed)


def prepare_block(state, w_first, gain_row):
    inverse = lax.rsqrt(jnp.mean(state * state, axis=-1, keepdims=True) + 1e-05)
    normed = (state * inverse * gain_row).astype(jnp.bfloat16)
    preact = jnp.dot(normed, w_first, preferred_element_type=jnp.float32)
    return (inverse, preact)


def finish_block(state, preact, w_second, decay_row):
    hidden = jax.nn.silu(preact).astype(jnp.bfloat16)
    return decay_row * state + jnp.dot(hidden, w_second, preferred_element_type=jnp.float32)


def backward_block(state, inverse, preact, upstream, w_first, w_second, gain_row, decay_row):
    grad_hidden = lax.dot_general(
        upstream.astype(jnp.bfloat16),
        w_second,
        (((1,), (1,)), ((), ())),
        preferred_element_type=jnp.float32,
    )
    sigma = jax.nn.sigmoid(preact)
    grad_pre = (grad_hidden * sigma * (1.0 + preact * (1.0 - sigma))).astype(jnp.bfloat16)
    grad_norm = lax.dot_general(
        grad_pre, w_first, (((1,), (1,)), ((), ())), preferred_element_type=jnp.float32
    )
    scaled = grad_norm * gain_row
    inner = jnp.mean(scaled * state, axis=-1, keepdims=True)
    return decay_row * upstream + inverse * scaled - state * inverse**3 * inner


def relax_forward(start, w_in, w_out, norm_gain, decay, want_end):
    state = start
    count = w_in.shape[0]
    states_list, inverse_list, preact_list = ([], [], [])
    for block in range(count):
        states_list.append(state)
        inverse, preact = prepare_block(state, w_in[block], norm_gain[block])
        inverse_list.append(inverse)
        preact_list.append(preact)
        if want_end or block + 1 < count:
            state = finish_block(state, preact, w_out[block], decay[block])
    return (state, states_list, inverse_list, preact_list)


def relax_backward(start, states, inverses, preacts, w_in, w_out, norm_gain, decay):
    adjoint = start
    count = w_in.shape[0]
    collected = [None] * count
    for block in reversed(range(count)):
        adjoint = backward_block(
            states[block],
            inverses[block],
            preacts[block],
            adjoint,
            w_in[block],
            w_out[block],
            norm_gain[block],
            decay[block],
        )
        collected[block] = adjoint
    return (adjoint, collected)


def compose(earlier, later):
    return (later[0] * earlier[0], later[0] * earlier[1] + later[1])


def shards(state_guess, adjoint_guess, w_in, w_out, norm_gain, decay):
    factor = jnp.prod(decay, axis=0)
    guess_state = state_guess[0]
    guess_adjoint = adjoint_guess[0]
    next_guess = shifted(guess_state, "depth", -1)
    prev_guess = shifted(guess_adjoint, "depth", 1)
    end_state, _, _, _ = relax_forward(guess_state, w_in, w_out, norm_gain, decay, True)
    correction = kernel_scan(factor, end_state - next_guess, False, 0)
    start = guess_state + correction
    _, states, inverses, preacts = relax_forward(start, w_in, w_out, norm_gain, decay, False)
    first_adjoint, _ = relax_backward(
        guess_adjoint, states, inverses, preacts, w_in, w_out, norm_gain, decay
    )
    eps = kernel_scan(factor, first_adjoint - prev_guess, True, 1)
    head = guess_adjoint + eps
    _, lambdas = relax_backward(head, states, inverses, preacts, w_in, w_out, norm_gain, decay)
    return (jnp.stack(states), jnp.stack(lambdas))


def solution(mesh):
    placed = (
        P("depth", None, None),
        P("depth", None, None),
        P("depth", None, None),
        P("depth", None, None),
        P("depth", None),
        P("depth", None),
    )
    return jax.shard_map(
        shards,
        mesh=mesh,
        in_specs=placed,
        out_specs=(P("depth", None, None), P("depth", None, None)),
        check_vma=False,
    )
```

```python
import functools

import jax
import jax.numpy as jnp
from jax import lax
from jax.experimental import pallas as pl
from jax.experimental.pallas import tpu as pltpu
from jax.sharding import PartitionSpec as P


def shifted(block, axis, distance):
    devices = range(lax.axis_size(axis))
    route = [(i - distance, i) for i in devices if i - distance in devices]
    return lax.ppermute(block, axis, route)


MESH = pl.DeviceIdType.MESH


def radices(groups):
    along_z = min(groups, 8)
    out = []
    for part in (along_z, groups // along_z):
        while part > 1:
            step = 2 if part % 8 == 0 else (4 if part % 4 == 0 else 2)
            out.append(step)
            part //= step
    return out


def group_kernel(size, reverse, pieces, packed_ref, out_ref, got, state, q_got, q_state, gathered, final, pair, sends, recvs):
    position = lax.axis_index("depth")
    order = size - 1 - position if reverse else position
    core, chip = (order % 2, order // 2)
    ring, group = (chip % 4, chip // 4)
    rows = out_ref.shape[0]
    half = packed_ref.shape[1] // 2
    groups = size // 8
    quarter = rows // 4
    step_rows = rows // pieces
    spans = [(rows, 8)] + [(k * step_rows, step_rows) for k in range(pieces)]
    levels = []
    width_now = 1
    for step in radices(groups):
        levels.append((width_now, list(range(1, step))))
        width_now *= step
    links = [(level, k) for level, (_, ks) in enumerate(levels) for k in ks]
    slot_c, slot_e, slot_f = (4, 5 + len(levels), 6 + len(levels))
    index = order % 8

    def device(q):
        q = lax.rem(q + 2 * size, size)
        return (size - 1 - q if reverse else q,)

    def in_ring(step):
        return order + 2 * ((ring + step + 4) % 4 - ring)

    partner = order + 1 - 2 * core
    source = order - 8 + 2 * (3 - ring)
    sinks = [order + 8 + 2 * (k - 3) for k in range(4)]
    targets = [order + 8 + 2 * (k - ring) for k in range(4)]
    targets += [in_ring(3), in_ring(-3)]
    targets += [order - 8 + 2 * (k - ring) for k in range(4)]
    for spread_width, ks in levels:
        targets += [order + 8 * k * spread_width for k in ks] + [order - 8 * k * spread_width for k in ks]
    targets += [order - index + (index + t) % 8 for t in range(1, 8)]
    targets += [order + 1, order - 1, order + 2, order - 2, order + 3, order - 3]
    barrier = pltpu.get_barrier_semaphore()
    for target in targets:
        pl.semaphore_signal(barrier, inc=1, device_id=device(target), device_id_type=MESH)
    last_of_ring = ring == 3
    pl.semaphore_wait(barrier, len(targets))

    started = []

    def copy(src, dst, slot, piece, target, start=True, keep=True, landing=None):
        handle = pltpu.make_async_remote_copy(
            src_ref=src,
            dst_ref=dst,
            send_sem=sends.at[slot, piece],
            recv_sem=recvs.at[slot, piece if landing is None else landing],
            device_id=device(target),
            device_id_type=MESH,
        )
        if start:
            handle.start()
        if start and keep:
            started.append(handle)
        return handle

    def block(ref, piece):
        first_row, count = spans[piece]
        return ref.at[pl.ds(first_row, count), :]

    first = core == 0
    factor_row = slice(rows, rows + 1)
    mine_ref = packed_ref.at[:, pl.ds(pl.multiple_of(core * half, half), half)]
    other_ref = packed_ref.at[:, pl.ds(pl.multiple_of((1 - core) * half, half), half)]
    pending = [copy(block(other_ref, k), block(got.at[0], k), 0, k, partner) for k in range(pieces + 1)]
    ahead = []
    for piece in range(pieces + 1):
        first_row, count = spans[piece]
        part = slice(first_row, first_row + count)
        pending[piece].wait_recv()
        came = got[0, part, :]
        mine = mine_ref[part, :]
        later = jnp.where(first, came, mine)
        earlier = jnp.where(first, mine, came)
        scale = jnp.where(first, got[0, factor_row, :], mine_ref[factor_row, :])
        state[0, part, :] = later * earlier if piece == 0 else later + scale * earlier
        ahead.append(
            [copy(block(state.at[0], piece), block(got.at[step], piece), step, piece, in_ring(step)) for step in (1, 2, 3)]
        )
    for piece in range(pieces + 1):
        first_row, count = spans[piece]
        part = slice(first_row, first_row + count)
        value = state[0, part, :]
        scale = state[0, factor_row, :]
        for step in (1, 2, 3):
            ahead[piece][step - 1].wait_recv()
            came = got[step, part, :]
            reach = ring >= step
            if piece == 0:
                value = jnp.where(reach, value * came, value)
            else:
                value = jnp.where(reach, value + scale * came, value)
                scale = jnp.where(reach, scale * got[step, factor_row, :], scale)
        state[2, part, :] = value

    sides = [copy(state.at[2], final.at[k], slot_f, k, order + 1 + k) for k in range(3)]
    sides.append(copy(mine_ref, pair, slot_f, 3, partner))

    def scatter(start):
        for k in range(4):
            for piece, (first_row, count, landing) in enumerate(((k * quarter, quarter, 0), (rows, 8, quarter))):
                handle = copy(
                    state.at[2].at[pl.ds(first_row, count), :],
                    q_got.at[0].at[pl.ds(landing, count), :],
                    slot_c,
                    2 * k + piece,
                    sinks[k],
                    start=start,
                    keep=False,
                    landing=piece,
                )
                if not start:
                    handle.wait_send()

    @pl.when(last_of_ring)
    def _():
        scatter(True)

    for k, piece_rows in ((0, (0, quarter)), (1, (quarter, 8))):
        copy(
            state.at[2].at[pl.ds(piece_rows[0], piece_rows[1]), :],
            q_got.at[0].at[pl.ds(piece_rows[0], piece_rows[1]), :],
            slot_c,
            k,
            source,
            start=False,
        ).wait_recv()
    incoming = q_got[0]
    is_head = group == 0
    identity = jnp.concatenate(
        [jnp.zeros((quarter, half), jnp.float32), jnp.ones((8, half), jnp.float32)], axis=0
    )
    q_state[0] = jnp.where(is_head, identity, incoming)
    landing = 1
    for level, (spread_width, ks) in enumerate(levels):
        arrivals = []
        for k in ks:
            arrivals.append((k, copy(q_state.at[level], q_got.at[landing], 5 + level, k - 1, order + 8 * k * spread_width), landing))
            landing += 1
        held = q_state[level]
        for k, handle, spot in arrivals:
            handle.wait_recv()
            came = q_got[spot]
            scale = held[quarter : quarter + 1, :]
            combined = jnp.concatenate([held[:quarter] + scale * came[:quarter], held[quarter:] * came[quarter:]], axis=0)
            held = jnp.where(group >= k * spread_width, combined, held)
        q_state[level + 1] = held
    depth = len(levels)
    prefix = q_state.at[depth].at[pl.ds(0, quarter), :]
    spread_copies = [copy(prefix, gathered.at[t - 1], slot_e, t - 1, order - index + (index + t) % 8) for t in range(1, 8)]
    for handle in sides + spread_copies:
        handle.wait_recv()
    at_start = ring == 0
    for t in range(8):
        owner = (index - t + 8) % 8
        owner_ring, owner_core = (owner // 2, owner % 2)
        band = pl.ds(pl.multiple_of(owner_ring * quarter, quarter), quarter)
        piece = q_state[depth, :quarter, :] if t == 0 else gathered[t - 1]
        left_side = owner_core == 0
        low = jnp.where(first, final[1, band, :], final[2, band, :])
        low_scale = jnp.where(first, final[1, factor_row, :], final[2, factor_row, :])
        high = jnp.where(first, final[0, band, :], final[1, band, :])
        high_scale = jnp.where(first, final[0, factor_row, :], final[1, factor_row, :])
        before = jnp.where(left_side, low, high)
        before_scale = jnp.where(left_side, low_scale, high_scale)
        behind = jnp.where(at_start, piece, before + before_scale * piece)
        element = jnp.where(left_side, pair[band, :], got[0, band, :])
        element_scale = jnp.where(left_side, pair[factor_row, :], got[0, factor_row, :])
        cols = pl.ds(pl.multiple_of(owner_core * half, half), half)
        out_ref[band, cols] = jnp.where(first, behind, element + element_scale * behind)
    for handle in started:
        handle.wait_send()

    @pl.when(last_of_ring)
    def _():
        scatter(False)


def kernel_scan(factor, offset, reverse, ident):
    size = lax.axis_size("depth")
    rows, width = offset.shape
    half = width // 2
    spread = jnp.broadcast_to(factor[None, :], (8, width))
    packed = jnp.concatenate([offset, spread], axis=0)
    groups = size // 8
    links = sum(step - 1 for step in radices(groups))
    levels = len(radices(groups))
    quarter = rows // 4
    return pl.pallas_call(
        functools.partial(group_kernel, size, reverse, 4),
        out_shape=jax.ShapeDtypeStruct((rows, width), jnp.float32),
        in_specs=[pl.BlockSpec(memory_space=pltpu.VMEM)],
        out_specs=pl.BlockSpec(memory_space=pltpu.VMEM),
        scratch_shapes=[
            pltpu.VMEM((4, rows + 8, half), jnp.float32),
            pltpu.VMEM((3, rows + 8, half), jnp.float32),
            pltpu.VMEM((links + 1, quarter + 8, half), jnp.float32),
            pltpu.VMEM((levels + 1, quarter + 8, half), jnp.float32),
            pltpu.VMEM((7, quarter, half), jnp.float32),
            pltpu.VMEM((3, rows + 8, half), jnp.float32),
            pltpu.VMEM((rows + 8, half), jnp.float32),
            pltpu.SemaphoreType.DMA((7 + levels, 8)),
            pltpu.SemaphoreType.DMA((7 + levels, 8)),
        ],
        compiler_params=pltpu.CompilerParams(collective_id=ident, has_side_effects=True),
    )(packed)


def prepare_block(state, w_first, gain_row):
    inverse = lax.rsqrt(jnp.mean(state * state, axis=-1, keepdims=True) + 1e-05)
    normed = (state * inverse * gain_row).astype(jnp.bfloat16)
    preact = jnp.dot(normed, w_first, preferred_element_type=jnp.float32)
    return (inverse, preact)


def finish_block(state, preact, w_second, decay_row):
    hidden = jax.nn.silu(preact).astype(jnp.bfloat16)
    return decay_row * state + jnp.dot(hidden, w_second, preferred_element_type=jnp.float32)


def backward_block(state, inverse, preact, upstream, w_first, w_second, gain_row, decay_row):
    grad_hidden = lax.dot_general(
        upstream.astype(jnp.bfloat16),
        w_second,
        (((1,), (1,)), ((), ())),
        preferred_element_type=jnp.float32,
    )
    sigma = jax.nn.sigmoid(preact)
    grad_pre = (grad_hidden * sigma * (1.0 + preact * (1.0 - sigma))).astype(jnp.bfloat16)
    grad_norm = lax.dot_general(
        grad_pre, w_first, (((1,), (1,)), ((), ())), preferred_element_type=jnp.float32
    )
    scaled = grad_norm * gain_row
    inner = jnp.mean(scaled * state, axis=-1, keepdims=True)
    return decay_row * upstream + inverse * scaled - state * inverse**3 * inner


def relax_forward(start, w_in, w_out, norm_gain, decay, want_end):
    state = start
    count = w_in.shape[0]
    states_list, inverse_list, preact_list = ([], [], [])
    for block in range(count):
        states_list.append(state)
        inverse, preact = prepare_block(state, w_in[block], norm_gain[block])
        inverse_list.append(inverse)
        preact_list.append(preact)
        if want_end or block + 1 < count:
            state = finish_block(state, preact, w_out[block], decay[block])
    return (state, states_list, inverse_list, preact_list)


def relax_backward(start, states, inverses, preacts, w_in, w_out, norm_gain, decay):
    adjoint = start
    count = w_in.shape[0]
    collected = [None] * count
    for block in reversed(range(count)):
        adjoint = backward_block(
            states[block],
            inverses[block],
            preacts[block],
            adjoint,
            w_in[block],
            w_out[block],
            norm_gain[block],
            decay[block],
        )
        collected[block] = adjoint
    return (adjoint, collected)


def compose(earlier, later):
    return (later[0] * earlier[0], later[0] * earlier[1] + later[1])


def shards(state_guess, adjoint_guess, w_in, w_out, norm_gain, decay):
    factor = jnp.prod(decay, axis=0)
    guess_state = state_guess[0]
    guess_adjoint = adjoint_guess[0]
    next_guess = shifted(guess_state, "depth", -1)
    prev_guess = shifted(guess_adjoint, "depth", 1)
    end_state, _, _, _ = relax_forward(guess_state, w_in, w_out, norm_gain, decay, True)
    correction = kernel_scan(factor, end_state - next_guess, False, 0)
    start = guess_state + correction
    _, states, inverses, preacts = relax_forward(start, w_in, w_out, norm_gain, decay, False)
    first_adjoint, _ = relax_backward(
        guess_adjoint, states, inverses, preacts, w_in, w_out, norm_gain, decay
    )
    eps = kernel_scan(factor, first_adjoint - prev_guess, True, 1)
    head = guess_adjoint + eps
    _, lambdas = relax_backward(head, states, inverses, preacts, w_in, w_out, norm_gain, decay)
    return (jnp.stack(states), jnp.stack(lambdas))


def solution(mesh):
    placed = (
        P("depth", None, None),
        P("depth", None, None),
        P("depth", None, None),
        P("depth", None, None),
        P("depth", None),
        P("depth", None),
    )
    return jax.shard_map(
        shards,
        mesh=mesh,
        in_specs=placed,
        out_specs=(P("depth", None, None), P("depth", None, None)),
        check_vma=False,
    )
```

```python
import functools

import jax
import jax.numpy as jnp
from jax import lax
from jax.experimental import pallas as pl
from jax.experimental.pallas import tpu as pltpu
from jax.sharding import PartitionSpec as P


def shifted(block, axis, distance):
    devices = range(lax.axis_size(axis))
    route = [(i - distance, i) for i in devices if i - distance in devices]
    return lax.ppermute(block, axis, route)


MESH = pl.DeviceIdType.MESH


def radices(groups):
    along_z = min(groups, 8)
    out = []
    for axis, part in enumerate((along_z, groups // along_z)):
        while part > 1:
            step = 2 if part % 8 == 0 or axis == 1 else (4 if part % 4 == 0 else 2)
            out.append(step)
            part //= step
    return out


def group_kernel(size, reverse, pieces, packed_ref, out_ref, got, state, q_got, q_state, gathered, final, pair, sends, recvs):
    position = lax.axis_index("depth")
    order = size - 1 - position if reverse else position
    core, chip = (order % 2, order // 2)
    ring, group = (chip % 4, chip // 4)
    rows = out_ref.shape[0]
    half = packed_ref.shape[1] // 2
    groups = size // 8
    quarter = rows // 4
    step_rows = rows // pieces
    spans = [(rows, 8)] + [(k * step_rows, step_rows) for k in range(pieces)]
    levels = []
    width_now = 1
    for step in radices(groups):
        levels.append((width_now, list(range(1, step))))
        width_now *= step
    links = [(level, k) for level, (_, ks) in enumerate(levels) for k in ks]
    slot_c, slot_e, slot_f = (3, 4 + len(levels), 5 + len(levels))
    index = order % 8

    def device(q):
        q = lax.rem(q + 2 * size, size)
        return (size - 1 - q if reverse else q,)

    def in_ring(step):
        return order + 2 * ((ring + step + 4) % 4 - ring)

    partner = order + 1 - 2 * core
    source = order - 8 + 2 * (3 - ring)
    sinks = [order + 8 + 2 * (k - 3) for k in range(4)]
    targets = [order + 8 + 2 * (k - ring) for k in range(4)]
    targets += [order - 8 + 2 * (k - ring) for k in range(4)]
    for spread_width, ks in levels:
        targets += [order + 8 * k * spread_width for k in ks] + [order - 8 * k * spread_width for k in ks]
    targets += [order - index + (index + t) % 8 for t in range(1, 8)]
    targets += [order + 1, order - 1, order + 2, order - 2, order + 3, order - 3]
    barrier = pltpu.get_barrier_semaphore()
    for target in targets:
        pl.semaphore_signal(barrier, inc=1, device_id=device(target), device_id_type=MESH)
    last_of_ring = ring == 3
    pl.semaphore_wait(barrier, len(targets))

    started = []

    def copy(src, dst, slot, piece, target, start=True, keep=True, landing=None):
        handle = pltpu.make_async_remote_copy(
            src_ref=src,
            dst_ref=dst,
            send_sem=sends.at[slot, piece],
            recv_sem=recvs.at[slot, piece if landing is None else landing],
            device_id=device(target),
            device_id_type=MESH,
        )
        if start:
            handle.start()
        if start and keep:
            started.append(handle)
        return handle

    def block(ref, piece):
        first_row, count = spans[piece]
        return ref.at[pl.ds(first_row, count), :]

    first = core == 0
    factor_row = slice(rows, rows + 1)
    mine_ref = packed_ref.at[:, pl.ds(pl.multiple_of(core * half, half), half)]
    other_ref = packed_ref.at[:, pl.ds(pl.multiple_of((1 - core) * half, half), half)]
    pending = [copy(block(other_ref, k), block(got.at[0], k), 0, k, partner) for k in range(pieces + 1)]
    for stage in range(3):
        following = []
        for piece in range(pieces + 1):
            first_row, count = spans[piece]
            part = slice(first_row, first_row + count)
            pending[piece].wait_recv()
            came = got[stage, part, :]
            if stage == 0:
                mine = mine_ref[part, :]
                later = jnp.where(first, came, mine)
                earlier = jnp.where(first, mine, came)
                scale = jnp.where(first, got[0, factor_row, :], mine_ref[factor_row, :])
                value = later * earlier if piece == 0 else later + scale * earlier
            else:
                held = state[stage - 1, part, :]
                scale = state[stage - 1, factor_row, :]
                combined = held * came if piece == 0 else held + scale * came
                value = jnp.where(ring >= stage, combined, held)
            state[stage, part, :] = value
            if stage < 2:
                step = 1 if stage == 0 else 2
                following.append(
                    copy(block(state.at[stage], piece), block(got.at[stage + 1], piece), stage + 1, piece, in_ring(step))
                )
        pending = following

    sides = [copy(state.at[2], final.at[k], slot_f, k, order + 1 + k) for k in range(3)]
    sides.append(copy(mine_ref, pair, slot_f, 3, partner))

    def scatter(start):
        for k in range(4):
            for piece, (first_row, count, landing) in enumerate(((k * quarter, quarter, 0), (rows, 8, quarter))):
                handle = copy(
                    state.at[2].at[pl.ds(first_row, count), :],
                    q_got.at[0].at[pl.ds(landing, count), :],
                    slot_c,
                    2 * k + piece,
                    sinks[k],
                    start=start,
                    keep=False,
                    landing=piece,
                )
                if not start:
                    handle.wait_send()

    @pl.when(last_of_ring)
    def _():
        scatter(True)

    for k, piece_rows in ((0, (0, quarter)), (1, (quarter, 8))):
        copy(
            state.at[2].at[pl.ds(piece_rows[0], piece_rows[1]), :],
            q_got.at[0].at[pl.ds(piece_rows[0], piece_rows[1]), :],
            slot_c,
            k,
            source,
            start=False,
        ).wait_recv()
    incoming = q_got[0]
    is_head = group == 0
    identity = jnp.concatenate(
        [jnp.zeros((quarter, half), jnp.float32), jnp.ones((8, half), jnp.float32)], axis=0
    )
    q_state[0] = jnp.where(is_head, identity, incoming)
    landing = 1
    for level, (spread_width, ks) in enumerate(levels):
        arrivals = []
        for k in ks:
            arrivals.append((k, copy(q_state.at[level], q_got.at[landing], 4 + level, k - 1, order + 8 * k * spread_width), landing))
            landing += 1
        held = q_state[level]
        for k, handle, spot in arrivals:
            handle.wait_recv()
            came = q_got[spot]
            scale = held[quarter : quarter + 1, :]
            combined = jnp.concatenate([held[:quarter] + scale * came[:quarter], held[quarter:] * came[quarter:]], axis=0)
            held = jnp.where(group >= k * spread_width, combined, held)
        q_state[level + 1] = held
    depth = len(levels)
    prefix = q_state.at[depth].at[pl.ds(0, quarter), :]
    spread_copies = [copy(prefix, gathered.at[t - 1], slot_e, t - 1, order - index + (index + t) % 8) for t in range(1, 8)]
    for handle in sides + spread_copies:
        handle.wait_recv()
    at_start = ring == 0
    for t in range(8):
        owner = (index - t + 8) % 8
        owner_ring, owner_core = (owner // 2, owner % 2)
        band = pl.ds(pl.multiple_of(owner_ring * quarter, quarter), quarter)
        piece = q_state[depth, :quarter, :] if t == 0 else gathered[t - 1]
        left_side = owner_core == 0
        low = jnp.where(first, final[1, band, :], final[2, band, :])
        low_scale = jnp.where(first, final[1, factor_row, :], final[2, factor_row, :])
        high = jnp.where(first, final[0, band, :], final[1, band, :])
        high_scale = jnp.where(first, final[0, factor_row, :], final[1, factor_row, :])
        before = jnp.where(left_side, low, high)
        before_scale = jnp.where(left_side, low_scale, high_scale)
        behind = jnp.where(at_start, piece, before + before_scale * piece)
        element = jnp.where(left_side, pair[band, :], got[0, band, :])
        element_scale = jnp.where(left_side, pair[factor_row, :], got[0, factor_row, :])
        cols = pl.ds(pl.multiple_of(owner_core * half, half), half)
        out_ref[band, cols] = jnp.where(first, behind, element + element_scale * behind)
    for handle in started:
        handle.wait_send()

    @pl.when(last_of_ring)
    def _():
        scatter(False)


def kernel_scan(factor, offset, reverse, ident):
    size = lax.axis_size("depth")
    rows, width = offset.shape
    half = width // 2
    spread = jnp.broadcast_to(factor[None, :], (8, width))
    packed = jnp.concatenate([offset, spread], axis=0)
    groups = size // 8
    links = sum(step - 1 for step in radices(groups))
    levels = len(radices(groups))
    quarter = rows // 4
    return pl.pallas_call(
        functools.partial(group_kernel, size, reverse, 4),
        out_shape=jax.ShapeDtypeStruct((rows, width), jnp.float32),
        in_specs=[pl.BlockSpec(memory_space=pltpu.VMEM)],
        out_specs=pl.BlockSpec(memory_space=pltpu.VMEM),
        scratch_shapes=[
            pltpu.VMEM((3, rows + 8, half), jnp.float32),
            pltpu.VMEM((3, rows + 8, half), jnp.float32),
            pltpu.VMEM((links + 1, quarter + 8, half), jnp.float32),
            pltpu.VMEM((levels + 1, quarter + 8, half), jnp.float32),
            pltpu.VMEM((7, quarter, half), jnp.float32),
            pltpu.VMEM((3, rows + 8, half), jnp.float32),
            pltpu.VMEM((rows + 8, half), jnp.float32),
            pltpu.SemaphoreType.DMA((6 + levels, 8)),
            pltpu.SemaphoreType.DMA((6 + levels, 8)),
        ],
        compiler_params=pltpu.CompilerParams(collective_id=ident, has_side_effects=True),
    )(packed)


def prepare_block(state, w_first, gain_row):
    inverse = lax.rsqrt(jnp.mean(state * state, axis=-1, keepdims=True) + 1e-05)
    normed = (state * inverse * gain_row).astype(jnp.bfloat16)
    preact = jnp.dot(normed, w_first, preferred_element_type=jnp.float32)
    return (inverse, preact)


def finish_block(state, preact, w_second, decay_row):
    hidden = jax.nn.silu(preact).astype(jnp.bfloat16)
    return decay_row * state + jnp.dot(hidden, w_second, preferred_element_type=jnp.float32)


def backward_block(state, inverse, preact, upstream, w_first, w_second, gain_row, decay_row):
    grad_hidden = lax.dot_general(
        upstream.astype(jnp.bfloat16),
        w_second,
        (((1,), (1,)), ((), ())),
        preferred_element_type=jnp.float32,
    )
    sigma = jax.nn.sigmoid(preact)
    grad_pre = (grad_hidden * sigma * (1.0 + preact * (1.0 - sigma))).astype(jnp.bfloat16)
    grad_norm = lax.dot_general(
        grad_pre, w_first, (((1,), (1,)), ((), ())), preferred_element_type=jnp.float32
    )
    scaled = grad_norm * gain_row
    inner = jnp.mean(scaled * state, axis=-1, keepdims=True)
    return decay_row * upstream + inverse * scaled - state * inverse**3 * inner


def relax_forward(start, w_in, w_out, norm_gain, decay, want_end):
    state = start
    count = w_in.shape[0]
    states_list, inverse_list, preact_list = ([], [], [])
    for block in range(count):
        states_list.append(state)
        inverse, preact = prepare_block(state, w_in[block], norm_gain[block])
        inverse_list.append(inverse)
        preact_list.append(preact)
        if want_end or block + 1 < count:
            state = finish_block(state, preact, w_out[block], decay[block])
    return (state, states_list, inverse_list, preact_list)


def relax_backward(start, states, inverses, preacts, w_in, w_out, norm_gain, decay):
    adjoint = start
    count = w_in.shape[0]
    collected = [None] * count
    for block in reversed(range(count)):
        adjoint = backward_block(
            states[block],
            inverses[block],
            preacts[block],
            adjoint,
            w_in[block],
            w_out[block],
            norm_gain[block],
            decay[block],
        )
        collected[block] = adjoint
    return (adjoint, collected)


def compose(earlier, later):
    return (later[0] * earlier[0], later[0] * earlier[1] + later[1])


def shards(state_guess, adjoint_guess, w_in, w_out, norm_gain, decay):
    factor = jnp.prod(decay, axis=0)
    guess_state = state_guess[0]
    guess_adjoint = adjoint_guess[0]
    next_guess = shifted(guess_state, "depth", -1)
    prev_guess = shifted(guess_adjoint, "depth", 1)
    end_state, _, _, _ = relax_forward(guess_state, w_in, w_out, norm_gain, decay, True)
    correction = kernel_scan(factor, end_state - next_guess, False, 0)
    start = guess_state + correction
    _, states, inverses, preacts = relax_forward(start, w_in, w_out, norm_gain, decay, False)
    first_adjoint, _ = relax_backward(
        guess_adjoint, states, inverses, preacts, w_in, w_out, norm_gain, decay
    )
    eps = kernel_scan(factor, first_adjoint - prev_guess, True, 1)
    head = guess_adjoint + eps
    _, lambdas = relax_backward(head, states, inverses, preacts, w_in, w_out, norm_gain, decay)
    return (jnp.stack(states), jnp.stack(lambdas))


def solution(mesh):
    placed = (
        P("depth", None, None),
        P("depth", None, None),
        P("depth", None, None),
        P("depth", None, None),
        P("depth", None),
        P("depth", None),
    )
    return jax.shard_map(
        shards,
        mesh=mesh,
        in_specs=placed,
        out_specs=(P("depth", None, None), P("depth", None, None)),
        check_vma=False,
    )
```
